32 devices in a mesh: ens: 2 (over y), seq: 4 (over z), mp: 2 (over x), sub: 2 (over core).
Axes of the slice: x: 2, y: 2, z: 4, core: 2. Of those that a mesh axis runs over, the one named last changes fastest.
Arguments:
- grid_latent: bfloat16 [16384, 1024], P(('ens', 'seq'), ('mp', 'sub')), parts along dimension 0, may hold values from -6 to 6
- grid_count: int32 [8], P(('ens', 'seq')), parts along dimension 0, may hold values from 1024 to 2048, as said below
- hidden_embed: bfloat16 [8192, 1024], P(('ens', 'seq'), ('mp', 'sub')), parts along dimension 0, may hold values from -6 to 6
- enc_src_rows: int32 [8, 32, 128], P(('ens', 'seq')), parts along dimension 0, may hold values from 0 to 2047, as said below
- enc_dst_rows: int32 [8, 32, 128], P(('ens', 'seq')), parts along dimension 0, may hold values from 0 to 1023
- enc_weight: float32 [8, 32, 128], P(('ens', 'seq')), parts along dimension 0, may hold values from 0.25 to 1
- dec_src_rows: int32 [8, 48, 128], P(('ens', 'seq')), parts along dimension 0, may hold values from 0 to 1023
- dec_dst_rows: int32 [8, 48, 128], P(('ens', 'seq')), parts along dimension 0, may hold values from 0 to 2047, as said below
- dec_weight: float32 [8, 48, 128], P(('ens', 'seq')), parts along dimension 0, may hold values from 0.25 to 1
- norm_gain: float32 [1024], replicated, may hold values from 0.1 to 1.9
- w_qkv: bfloat16 [1024, 3072], P(None, ('mp', 'sub'))
- w_out: bfloat16 [1024, 1024], P(('mp', 'sub')), may hold values from -0.1875 to 0.1875
- w_up: bfloat16 [1024, 4096], P(None, ('mp', 'sub')), may hold values from -0.1875 to 0.1875
- up_exp: int32 [4096], P(('mp', 'sub')), may hold values from -1 to 1
- w_down: bfloat16 [4096, 1024], P(('mp', 'sub')), may hold values from -0.09375 to 0.09375
- down_exp: int32 [1024], replicated, may hold values from -1 to 1
Outputs:
- hidden_out: bfloat16 [8192, 1024], P(('ens', 'seq'), ('mp', 'sub')), parts along dimension 0
- grid_out: bfloat16 [16384, 1024], P(('ens', 'seq'), ('mp', 'sub')), parts along dimension 0
The draws below stay inside these ranges and needn't reach their ends.
There are 2 independent parts, one for each index of `ens`. The reference program is written for one: setup_inputs(seed, part) draws one part's arguments, and reference() takes and returns one part's arrays. A program takes and returns all parts, laid end to end along the dimension named above; an argument that names none is the same for every part. Nothing has to cross between parts.
Inputs may be any that keep to these rules, and one draw needn't show every extreme that they name: `grid_count`: each block holds between 1024 and 2048 live grid nodes; some block holds exactly 2048. `enc_src_rows`: each source row is below grid_count of its sending block s. `dec_dst_rows`: each destination row is below grid_count of its receiving block d.
All inputs are finite; a program needn't handle non-finite values.
Results may differ from the reference program's by a relative error of at most 0.013.
Values may be sent and summed in bfloat16 or wider, within the bound.
No kernel may reach another device: no remote copies, remote signals or barrier semaphores. Data moves between devices by JAX's collectives and lax.ppermute only.
A program may use at most 128 MiB of HBM per device.

```python
import math
import jax
import jax.numpy as jnp
from jax import lax

D = 1024
HEADS = 16
HD = 64
FFW = 4096
WIN = 512
TILE = 128
ESIDE = 4
ELOCAL = 24
DSIDE = 4
DLOCAL = 40
HID_DEV = 1024
GCAP = 2048
ETILES = 32
DTILES = 48
HID_TOTAL = 4096
GRID = 8192
N_SEQ = 4
N_MP = 2
N_SUB = 2


def owner_counts(key):
    counts = jax.random.randint(jax.random.fold_in(key, 101), (N_SEQ,), GCAP // 2, GCAP + 1)
    full_owner = jax.random.randint(jax.random.fold_in(key, 102), (), 0, N_SEQ)
    return jnp.where(jnp.arange(N_SEQ) == full_owner, GCAP, counts).astype(jnp.int32)


def draw_grid_count(key, part):
    return owner_counts(key)


def draw_enc_src_rows(key, part):
    limits = owner_counts(key)[:, None, None]
    return jax.random.randint(jax.random.fold_in(key, 103), (N_SEQ, ELOCAL + 2 * ESIDE, TILE), 0, limits).astype(jnp.int32)


def draw_dec_dst_rows(key, part):
    limits = owner_counts(key)[:, None, None]
    return jax.random.randint(jax.random.fold_in(key, 104), (N_SEQ, DLOCAL + 2 * DSIDE, TILE), 0, limits).astype(jnp.int32)


def draw_w_qkv(key, part):
    base = jax.random.normal(jax.random.fold_in(key, 111), (D, HEADS, 3, HD), jnp.float32) * D ** (-0.5)
    return base.reshape(D, 3 * D).astype(jnp.bfloat16)


def touch_ends(array, key, low, largest):
    longest = array.shape.index(max(array.shape))
    spots = []
    for shift in (0, 1):
        where = [jax.random.randint(jax.random.fold_in(key, axis), (), 0, length) for axis, length in enumerate(array.shape)]
        where[longest] = (where[longest] + shift) % array.shape[longest]
        spots.append(tuple(where))
    return array.at[spots[0]].set(low).at[spots[1]].set(largest)


def block_scale(stream_key, shape, cuts, low, top_value):
    factor_of, own = 1.0, jax.random.fold_in(stream_key, 6)
    for axis_at, parts in cuts:
        draws = jnp.exp(jax.random.uniform(jax.random.fold_in(own, axis_at), (parts,), jnp.float32, low / len(cuts), top_value / len(cuts)))
        factor_of = factor_of * jnp.repeat(draws, shape[axis_at] // parts).reshape([-1 if axis == axis_at else 1 for axis in range(len(shape))])
    return factor_of


def noise(rng, shape, spread, bound, cuts=(), kind=jnp.bfloat16):
    entries = spread * jax.random.normal(rng, shape, jnp.float32)
    if cuts:
        entries = entries * block_scale(rng, shape, cuts, -0.22, 0.18)
    return jnp.clip(entries, -bound, bound).astype(kind)


def setup_inputs(seed: int = 0, part: int = 0) -> dict:
    key_list = jax.random.split(jax.random.key(seed), 17)
    part_splits = jax.random.split(jax.random.fold_in(key_list[16], part), 17)
    return {
        "grid_latent": noise(part_splits[0], (GRID, D), 1.0, 6.0, ((0, 4), (1, 4))),
        "grid_count": draw_grid_count(jax.random.fold_in(jax.random.fold_in(key_list[16], part), 71), part),
        "hidden_embed": noise(part_splits[2], (HID_TOTAL, D), 1.0, 6.0, ((0, 4), (1, 4))),
        "enc_src_rows": draw_enc_src_rows(jax.random.fold_in(jax.random.fold_in(key_list[16], part), 71), part),
        "enc_dst_rows": touch_ends(jax.random.randint(part_splits[4], (N_SEQ, ETILES, TILE), 0, HID_DEV), jax.random.fold_in(part_splits[4], 1), 0, HID_DEV - 1).astype(jnp.int32),
        "enc_weight": jnp.clip(jnp.exp(math.log(1.0) - 1.3862944 * jax.random.uniform(part_splits[5], (N_SEQ, ETILES, TILE), jnp.float32) ** block_scale(part_splits[5], (N_SEQ, ETILES, TILE), ((0, 4),), -0.2, 0.2)), 0.25, 1.0),
        "dec_src_rows": touch_ends(jax.random.randint(part_splits[6], (N_SEQ, DTILES, TILE), 0, HID_DEV), jax.random.fold_in(part_splits[6], 1), 0, HID_DEV - 1).astype(jnp.int32),
        "dec_dst_rows": draw_dec_dst_rows(jax.random.fold_in(jax.random.fold_in(key_list[16], part), 71), part),
        "dec_weight": jnp.clip(jnp.exp(math.log(1.0) - 1.3862944 * jax.random.uniform(part_splits[8], (N_SEQ, DTILES, TILE), jnp.float32) ** block_scale(part_splits[8], (N_SEQ, DTILES, TILE), ((0, 4),), -0.2, 0.2)), 0.25, 1.0),
        "norm_gain": jnp.clip(1.0 + 0.18 * jax.random.normal(key_list[9], (D,), jnp.float32), 0.1, 1.9),
        "w_qkv": draw_w_qkv(jax.random.fold_in(key_list[16], 71), part),
        "w_out": noise(key_list[11], (D, D), D ** -0.5, 0.1875, ((0, 4),)),
        "w_up": noise(key_list[12], (D, FFW), D ** -0.5, 0.1875, ((1, 4),)),
        "up_exp": touch_ends(jax.random.randint(key_list[13], (FFW,), -1, 2), jax.random.fold_in(key_list[13], 1), -1, 1).astype(jnp.int32),
        "w_down": noise(key_list[14], (FFW, D), FFW ** -0.5, 0.09375, ((0, 4),)),
        "down_exp": touch_ends(jax.random.randint(key_list[15], (D,), -1, 2), jax.random.fold_in(key_list[15], 1), -1, 1).astype(jnp.int32),
    }


def to_half(values):
    return lax.optimization_barrier(values.astype(jnp.bfloat16))

def norm_rows(rows, norm_gain):
    values = rows.astype(jnp.float32)
    row_mean = lax.optimization_barrier(jnp.mean(values, axis=-1, keepdims=True))
    centered = values - row_mean
    row_var = lax.optimization_barrier(jnp.mean(centered * centered, axis=-1, keepdims=True))
    return to_half(centered * lax.rsqrt(row_var + 1e-05) * norm_gain.astype(jnp.float32)[None, :])

def edge_sum(source, src_rows, dst_rows, weights, src_block, dst_block, side):
    blocks = N_SEQ
    width = side * TILE
    block_ids = jnp.arange(blocks, dtype=jnp.int32)
    src = src_rows.reshape(blocks, -1) + (block_ids * src_block)[:, None]
    wts = weights.reshape(blocks, -1)
    dst = dst_rows.reshape(blocks, -1) + (block_ids * dst_block)[:, None]
    left_src = jnp.roll(src[:, width:2 * width], 1, axis=0)
    left_wts = jnp.where((block_ids > 0)[:, None], jnp.roll(wts[:, width:2 * width], 1, axis=0), 0.0)
    right_src = jnp.roll(src[:, :width], -1, axis=0)
    right_wts = jnp.where((block_ids < blocks - 1)[:, None], jnp.roll(wts[:, :width], -1, axis=0), 0.0)
    arr_src = jnp.concatenate([left_src, right_src, src[:, 2 * width:]], axis=1).astype(jnp.int32)
    arr_wts = jnp.concatenate([left_wts, right_wts, wts[:, 2 * width:]], axis=1)

    def add_block(total, pieces):
        src_part, dst_part, weight_part = pieces
        picked = jnp.take(source, src_part, axis=0).astype(jnp.float32) * weight_part[:, None]
        return (total.at[dst_part].add(to_half(picked).astype(jnp.float32)), None)
    start = jnp.zeros((dst_block * blocks, source.shape[1]), jnp.float32)
    total, _ = lax.scan(add_block, start, (arr_src, dst, arr_wts))
    return total

def reference(grid_latent, grid_count, hidden_embed, enc_src_rows, enc_dst_rows, enc_weight, dec_src_rows, dec_dst_rows, dec_weight, norm_gain, w_qkv, w_out, w_up, up_exp, w_down, down_exp):
    blocks = N_SEQ
    hidden_total = HID_DEV * blocks
    encoded = edge_sum(grid_latent, enc_src_rows, enc_dst_rows, enc_weight, GCAP, HID_DEV, ESIDE)
    latent = to_half(hidden_embed.astype(jnp.float32) + encoded)
    normed = norm_rows(latent, norm_gain)
    qkv = jnp.dot(normed, w_qkv, preferred_element_type=jnp.float32).reshape(hidden_total, HEADS, 3, HD)
    queries = to_half(qkv[:, :, 0, :])
    keys = to_half(qkv[:, :, 1, :])
    values = to_half(qkv[:, :, 2, :])
    padding = jnp.zeros((WIN, HEADS, HD), jnp.bfloat16)
    keys_pad = jnp.concatenate([padding, keys, padding], axis=0)
    values_pad = jnp.concatenate([padding, values, padding], axis=0)
    query_rows = min(512, HID_DEV)
    span = query_rows + 2 * WIN
    scale = HD ** (-0.5)

    def attend_block(index):
        start = (index * query_rows).astype(jnp.int32)
        query_block = lax.dynamic_slice_in_dim(queries, start, query_rows, 0).astype(jnp.float32)
        key_block = lax.dynamic_slice_in_dim(keys_pad, start, span, 0).astype(jnp.float32)
        value_block = lax.dynamic_slice_in_dim(values_pad, start, span, 0).astype(jnp.float32)
        scores = jnp.einsum('qhd,khd->hqk', query_block, key_block) * scale
        query_pos = start + jnp.arange(query_rows, dtype=jnp.int32)
        key_pos = start - WIN + jnp.arange(span, dtype=jnp.int32)
        allowed = (jnp.abs(query_pos[:, None] - key_pos[None, :]) <= WIN) & (key_pos[None, :] >= 0) & (key_pos[None, :] < hidden_total)
        scores = jnp.where(allowed[None, :, :], scores, -1e+30)
        peak = lax.optimization_barrier(jnp.max(scores, axis=-1, keepdims=True))
        expo = jnp.exp(scores - peak)
        attn_weights = to_half(expo / lax.optimization_barrier(jnp.sum(expo, axis=-1, keepdims=True))).astype(jnp.float32)
        return to_half(jnp.einsum('hqk,khd->qhd', attn_weights, value_block))
    attended = lax.map(attend_block, jnp.arange(hidden_total // query_rows, dtype=jnp.int32)).reshape(hidden_total, D)
    up_proj = jnp.dot(normed, w_up, preferred_element_type=jnp.float32) * jnp.exp2(up_exp.astype(jnp.float32))[None, :]
    activated = to_half(jax.nn.gelu(up_proj, approximate=False))
    down_scale = jnp.exp2(down_exp.astype(jnp.float32))[None, :]
    shards = N_MP * N_SUB
    head_cols = D // shards
    unit_cols = FFW // shards
    summed = jnp.zeros((hidden_total, D), jnp.float32)
    for shard in range(shards):
        attn_part = jnp.dot(attended[:, shard * head_cols:(shard + 1) * head_cols], w_out[shard * head_cols:(shard + 1) * head_cols], preferred_element_type=jnp.float32)
        mlp_part = jnp.dot(activated[:, shard * unit_cols:(shard + 1) * unit_cols], w_down[shard * unit_cols:(shard + 1) * unit_cols], preferred_element_type=jnp.float32) * down_scale
        summed = summed + to_half(attn_part + mlp_part).astype(jnp.float32)
    hidden_out = to_half(latent.astype(jnp.float32) + summed)
    decoded = edge_sum(hidden_out, dec_src_rows, dec_dst_rows, dec_weight, HID_DEV, GCAP, DSIDE)
    live_rows = (jnp.arange(GCAP, dtype=jnp.int32)[None, :] < grid_count[:, None]).reshape(-1)
    grid_out = jnp.where(live_rows[:, None], grid_latent.astype(jnp.float32) + decoded, 0.0).astype(jnp.bfloat16)
    return (hidden_out.astype(jnp.bfloat16), grid_out)
```

```python
import functools

import jax
import jax.numpy as jnp
from jax import lax
from jax.experimental import pallas as pl
from jax.experimental.pallas import tpu as pltpu
from jax.sharding import PartitionSpec as P

HD = 64
WIN = 512
TILE = 128
ESIDE = 4
DSIDE = 4
STEP = 4
NEG = -1e30
BF = jnp.bfloat16
F32 = jnp.float32


def call(body, outs, args, flops, scratch=(), name=None):
    moved = sum(a.size * a.dtype.itemsize for a in args)
    moved += sum(o.size * o.dtype.itemsize for o in outs)
    return pl.pallas_call(
        body,
        out_shape=tuple(outs),
        in_specs=[pl.BlockSpec(memory_space=pltpu.VMEM)] * len(args),
        out_specs=tuple(pl.BlockSpec(memory_space=pltpu.VMEM) for _ in outs),
        scratch_shapes=list(scratch),
        cost_estimate=pl.CostEstimate(flops=flops, bytes_accessed=moved, transcendentals=0),
        compiler_params=pltpu.CompilerParams(vmem_limit_bytes=56 * 1024 * 1024),
        name=name,
    )(*args)


def column(row):
    return jnp.transpose(jnp.broadcast_to(row, (TILE, TILE)))


def picks(rows_ref, first, source_rows):
    cols = jnp.concatenate([column(rows_ref[pl.ds(first + i, 1), :]) for i in range(STEP)], axis=0)
    cols = cols.astype(jnp.int16)
    lane = lax.broadcasted_iota(jnp.int32, cols.shape, 1).astype(jnp.int16)
    tiles = []
    for j in range(source_rows // TILE):
        hit = cols == lane + jnp.int16(j * TILE)
        tiles.append(jnp.where(hit, jnp.ones_like(cols, BF), jnp.zeros_like(cols, BF)))
    return jnp.concatenate(tiles, axis=1)


def lands(rows_ref, first, target_rows):
    tiles = []
    spot = lax.broadcasted_iota(jnp.int32, (target_rows, TILE), 0).astype(jnp.int16)
    for i in range(STEP):
        row = jnp.broadcast_to(rows_ref[pl.ds(first + i, 1), :], (target_rows, TILE)).astype(jnp.int16)
        tiles.append(jnp.where(row == spot, jnp.ones_like(spot, BF), jnp.zeros_like(spot, BF)))
    return jnp.concatenate(tiles, axis=1)


def messages(src_ref, weight_ref, first, source_ref):
    picked = jnp.dot(
        picks(src_ref, first, source_ref.shape[0]), source_ref[...], preferred_element_type=F32
    )
    scale = jnp.concatenate([column(weight_ref[pl.ds(first + i, 1), :]) for i in range(STEP)], axis=0)
    scale = jnp.concatenate([scale] * (picked.shape[1] // TILE), axis=1)
    return (picked * scale).astype(BF)


def side_body(src_ref, weight_ref, source_ref, *outs):
    for side, out in enumerate(outs):
        for k in range(out.shape[0] // (STEP * TILE)):
            first = (side * out.shape[0]) // TILE + k * STEP
            out[k * STEP * TILE : (k + 1) * STEP * TILE, :] = messages(
                src_ref, weight_ref, first, source_ref
            )


def local_body(start, src_ref, dst_ref, weight_ref, source_ref, total_ref):
    total_ref[...] = jnp.zeros_like(total_ref)

    def step(k, carry):
        first = start + k * STEP
        moved = messages(src_ref, weight_ref, first, source_ref)
        total_ref[...] += jnp.dot(
            lands(dst_ref, first, total_ref.shape[0]), moved, preferred_element_type=F32
        )
        return carry

    lax.fori_loop(0, (src_ref.shape[0] - start) // STEP, step, 0)


def arrived(dst_ref, left_ref, right_ref, target_rows):
    total = jnp.dot(lands(dst_ref, 0, target_rows), left_ref[...], preferred_element_type=F32)
    return total + jnp.dot(
        lands(dst_ref, STEP, target_rows), right_ref[...], preferred_element_type=F32
    )


def latent_body(dst_ref, left_ref, right_ref, total_ref, embed_ref, out_ref):
    got = arrived(dst_ref, left_ref, right_ref, total_ref.shape[0]) + total_ref[...]
    out_ref[...] = (embed_ref[...].astype(F32) + got).astype(BF)


def grid_body(count_ref, dst_ref, left_ref, right_ref, total_ref, grid_ref, out_ref):
    got = arrived(dst_ref, left_ref, right_ref, total_ref.shape[0]) + total_ref[...]
    row = lax.broadcasted_iota(jnp.int32, got.shape, 0)
    value = grid_ref[...].astype(F32) + got
    out_ref[...] = jnp.where(row < count_ref[0, 0], value, 0.0).astype(BF)


def sent(edge_src, edge_weight, source, side):
    width = side * TILE
    out = jax.ShapeDtypeStruct((width, source.shape[1]), BF)
    flops = 4 * width * source.size
    to_left, to_right = call(side_body, (out, out), (edge_src, edge_weight, source), flops, name="side")
    count = lax.axis_size("seq")
    up = [(i, i + 1) for i in range(count - 1)]
    down = [(i + 1, i) for i in range(count - 1)]
    from_left = lax.ppermute(to_right, "seq", up)
    from_right = lax.ppermute(to_left, "seq", down)
    return from_left, from_right


def local(edge_src, edge_dst, edge_weight, source, target_rows, side):
    start = 2 * side
    edges = (edge_src.shape[0] - start) * TILE
    out = jax.ShapeDtypeStruct((target_rows, source.shape[1]), F32)
    flops = 2 * edges * source.shape[1] * (source.shape[0] + target_rows)
    (total,) = call(
        functools.partial(local_body, start),
        (out,),
        (edge_src, edge_dst, edge_weight, source),
        flops,
        name="local",
    )
    return total


def power(exponent):
    return jnp.where(exponent > 0, 2.0, jnp.where(exponent < 0, 0.5, 1.0)).astype(F32)


def place(step, parts):
    if parts == 1:
        return 0
    mp = lax.axis_index("mp")
    sub = lax.axis_index("sub")
    mp = mp if step < 2 else 1 - mp
    sub = sub if step % 2 == 0 else 1 - sub
    return 2 * mp + sub


def qkv_body(parts, *refs):
    pieces, (gain_ref, w_ref, normed_ref, q_ref, kv_ref) = refs[:parts], refs[parts:]
    rows, width = pieces[0].shape
    total = width * parts
    block = min(256, rows)
    lane = lax.broadcasted_iota(jnp.int32, (block, TILE), 1)

    def step(k, carry):
        at = pl.ds(pl.multiple_of(k * block, block), block)
        values = [p[at, :].astype(F32) for p in pieces]
        mean = sum(jnp.sum(v, axis=1, keepdims=True) for v in values) / total
        values = [v - mean for v in values]
        var = sum(jnp.sum(v * v, axis=1, keepdims=True) for v in values) / total
        scale = lax.rsqrt(var + 1e-05)
        for i, v in enumerate(values):
            cols = pl.ds(pl.multiple_of(place(i, parts) * width, width), width)
            normed_ref[at, cols] = (v * scale * gain_ref[:, cols]).astype(BF)
        out = jnp.dot(normed_ref[at, :], w_ref[...], preferred_element_type=F32)
        for pair in range(q_ref.shape[1] // TILE):
            a, b, c = [out[:, (3 * pair + i) * TILE : (3 * pair + i + 1) * TILE] for i in range(3)]
            q = pltpu.roll(jnp.where(lane < HD, a, b), HD, 1)
            q_ref[at, pair * TILE : (pair + 1) * TILE] = q.astype(BF)
            kv_ref[at, 2 * pair * TILE : (2 * pair + 1) * TILE] = jnp.where(lane < HD, b, a).astype(BF)
            kv_ref[at, (2 * pair + 1) * TILE : (2 * pair + 2) * TILE] = c.astype(BF)
        return carry

    lax.fori_loop(0, rows // block, step, 0)


def up_body(normed_ref, w_ref, exp_ref, out_ref):
    rows = normed_ref.shape[0]
    block = min(256, rows)
    cols = min(512, w_ref.shape[1])

    def step(k, carry):
        at = pl.ds(pl.multiple_of(k * block, block), block)
        for c in range(w_ref.shape[1] // cols):
            sl = slice(c * cols, (c + 1) * cols)
            up = jnp.dot(normed_ref[at, :], w_ref[:, sl], preferred_element_type=F32)
            up = up * power(exp_ref[:, sl])
            out_ref[at, sl] = (0.5 * up * (1.0 + lax.erf(up * 0.7071067811865476))).astype(BF)
        return carry

    lax.fori_loop(0, rows // block, step, 0)


def attend_body(where, q_ref, before_ref, here_ref, after_ref, out_ref):
    rows = q_ref.shape[0]
    block = 256
    lane = lax.broadcasted_iota(jnp.int32, (block, TILE), 1)
    i = lax.broadcasted_iota(jnp.int32, (block, block), 0)
    j = lax.broadcasted_iota(jnp.int32, (block, block), 1)
    seq = lax.axis_index("seq")
    before_ok = jnp.logical_or(where != 0, seq > 0)
    after_ok = jnp.logical_or(where != 1, seq < lax.axis_size("seq") - 1)
    before_bias = jnp.where(before_ok, 0.0, NEG).astype(F32)
    after_bias = jnp.where(after_ok, 0.0, NEG).astype(F32)
    low = jnp.where(j >= i, before_bias, NEG)
    high = jnp.where(j <= i, after_bias, NEG)
    contract = (((1,), (1,)), ((), ()))
    n = WIN // block
    for pair in range(q_ref.shape[1] // TILE):
        pair_cols = slice(pair * TILE, (pair + 1) * TILE)
        for b in range(rows // block):
            q2 = q_ref[b * block : (b + 1) * block, pair_cols]
            outs = []
            for half in range(2):
                cols = slice((2 * pair + half) * TILE, (2 * pair + half + 1) * TILE)
                keep = (lane >= HD) if half == 0 else (lane < HD)
                q = jnp.where(keep, q2 * BF(HD**-0.5), jnp.zeros_like(q2))
                keys = []
                for t in range(b, b + 2 * n + 1):
                    ref = (before_ref, here_ref, after_ref)[t // n]
                    keys.append((t, ref[(t % n) * block : (t % n + 1) * block, cols]))
                scores = []
                for t, key in keys:
                    s = lax.dot_general(q, key, contract, preferred_element_type=F32)
                    if t == b:
                        s = s + low
                    elif t == b + 2 * n:
                        s = s + high
                    elif t < n and where == 0:
                        s = s + before_bias
                    elif t >= 2 * n and where == 1:
                        s = s + after_bias
                    scores.append(s)
                peak = scores[0]
                for s in scores[1:]:
                    peak = jnp.maximum(peak, s)
                peak = jnp.max(peak, axis=1, keepdims=True)
                probs = [jnp.exp(s - peak) for s in scores]
                total = probs[0]
                for p in probs[1:]:
                    total = total + p
                total = jnp.sum(total, axis=1, keepdims=True)
                mixed = jnp.dot(
                    jnp.concatenate([p.astype(BF) for p in probs], axis=1),
                    jnp.concatenate([key for _, key in keys], axis=0),
                    preferred_element_type=F32,
                )
                outs.append(mixed / total)
            out_ref[b * block : (b + 1) * block, pair_cols] = jnp.where(
                lane < HD, outs[0], outs[1]
            ).astype(BF)


def down_body(parts, att_ref, act_ref, w_out_ref, w_down_ref, exp_ref, *outs):
    rows = att_ref.shape[0]
    width = w_out_ref.shape[1] // parts
    block = min(256, rows)

    def step(k, carry):
        at = pl.ds(pl.multiple_of(k * block, block), block)
        for i in range(parts):
            cols = pl.ds(pl.multiple_of(place(i, parts) * width, width), width)
            mlp = jnp.dot(act_ref[at, :], w_down_ref[:, cols], preferred_element_type=F32)
            att = jnp.dot(att_ref[at, :], w_out_ref[:, cols], preferred_element_type=F32)
            part = (att + mlp * power(exp_ref[:, cols])).astype(BF)
            outs[i][at, :] = part
        return carry

    lax.fori_loop(0, rows // block, step, 0)


SWAP = [(0, 1), (1, 0)]


def gather(rows, split):
    if not split:
        return [lax.all_gather(rows, ("mp", "sub"), axis=1, tiled=True)]
    far = lax.ppermute(rows, "mp", SWAP)
    near = lax.ppermute(rows, "sub", SWAP)
    both = lax.ppermute(far, "sub", SWAP)
    return [rows, near, far, both]


def reduce_parts(latent, parts, split):
    if not split:
        total = lax.psum_scatter(parts[0], ("mp", "sub"), scatter_dimension=1, tiled=True)
        return (latent.astype(F32) + total.astype(F32)).astype(BF)
    own, near, far, both = parts
    far_got = lax.ppermute(both, "sub", SWAP)
    near_got = lax.ppermute(near, "sub", SWAP)
    far_sum = (far.astype(F32) + far_got.astype(F32)).astype(BF)
    got = lax.ppermute(far_sum, "mp", SWAP)
    total = own.astype(F32) + near_got.astype(F32) + got.astype(F32)
    return (latent.astype(F32) + total).astype(BF)


def shards(
    grid_latent,
    grid_count,
    hidden_embed,
    enc_src_rows,
    enc_dst_rows,
    enc_weight,
    dec_src_rows,
    dec_dst_rows,
    dec_weight,
    norm_gain,
    w_qkv,
    w_out,
    w_up,
    up_exp,
    w_down,
    down_exp,
):
    split = lax.axis_size("mp") == 2 and lax.axis_size("sub") == 2
    parts = 4 if split else 1
    count = lax.axis_size("seq")
    up = [(i, i + 1) for i in range(count - 1)]
    down = [(i + 1, i) for i in range(count - 1)]
    hid_rows, features = hidden_embed.shape
    full = w_qkv.shape[0]
    heads = w_qkv.shape[1] // (3 * HD)
    units = w_up.shape[1]
    src, dst, wts = enc_src_rows[0], enc_dst_rows[0], enc_weight[0]
    from_left, from_right = sent(src, wts, grid_latent, ESIDE)
    total = local(src, dst, wts, grid_latent, hid_rows, ESIDE)
    (latent,) = call(
        latent_body,
        (jax.ShapeDtypeStruct(hidden_embed.shape, BF),),
        (dst, from_left, from_right, total, hidden_embed),
        4 * ESIDE * TILE * hid_rows * features,
        name="latent",
    )
    chunks = []
    rows = WIN
    for c in range(hid_rows // rows):
        part = latent[c * rows : (c + 1) * rows]
        pieces = gather(part, split)
        normed, q, kv = call(
            functools.partial(qkv_body, parts),
            (
                jax.ShapeDtypeStruct((rows, full), BF),
                jax.ShapeDtypeStruct((rows, heads * HD), BF),
                jax.ShapeDtypeStruct((rows, 2 * heads * HD), BF),
            ),
            (*pieces, norm_gain[None, :], w_qkv),
            2 * rows * w_qkv.size,
            name="qkv",
        )
        chunks.append((part, normed, q, kv))
    kvs = [chunk[3] for chunk in chunks]
    kvs = [
        lax.ppermute(kvs[-1], "seq", up),
        *kvs,
        lax.ppermute(kvs[0], "seq", down),
    ]
    hidden = []
    for c, (part, normed, q, _) in enumerate(chunks):
        (activated,) = call(
            up_body,
            (jax.ShapeDtypeStruct((rows, units), BF),),
            (normed, w_up, up_exp[None, :]),
            2 * rows * w_up.size,
            name="up",
        )
        where = 0 if c == 0 else (1 if c == len(chunks) - 1 else 2)
        (attended,) = call(
            functools.partial(attend_body, where),
            (jax.ShapeDtypeStruct((rows, heads * HD), BF),),
            (q, *kvs[c : c + 3]),
            4 * rows * 3 * WIN * heads * HD,
            name="attend",
        )
        outs = call(
            functools.partial(down_body, parts),
            [jax.ShapeDtypeStruct((rows, full // parts), BF)] * parts,
            (attended, activated, w_out, w_down, down_exp[None, :]),
            2 * rows * (w_out.size + w_down.size),
            name="down",
        )
        hidden.append(reduce_parts(part, outs, split))
    hidden_out = jnp.concatenate(hidden, axis=0)
    src, dst, wts = dec_src_rows[0], dec_dst_rows[0], dec_weight[0]
    from_left, from_right = sent(src, wts, hidden_out, DSIDE)
    total = local(src, dst, wts, hidden_out, grid_latent.shape[0], DSIDE)
    (grid_out,) = call(
        grid_body,
        (jax.ShapeDtypeStruct(grid_latent.shape, BF),),
        (grid_count[None, :], dst, from_left, from_right, total, grid_latent),
        4 * DSIDE * TILE * grid_latent.size,
        name="grid",
    )
    return (hidden_out, grid_out)


def solution(mesh):
    placed = (
        P(("ens", "seq"), ("mp", "sub")),
        P(("ens", "seq")),
        P(("ens", "seq"), ("mp", "sub")),
        P(("ens", "seq"), None, None),
        P(("ens", "seq"), None, None),
        P(("ens", "seq"), None, None),
        P(("ens", "seq"), None, None),
        P(("ens", "seq"), None, None),
        P(("ens", "seq"), None, None),
        P(),
        P(None, ("mp", "sub")),
        P(("mp", "sub"), None),
        P(None, ("mp", "sub")),
        P(("mp", "sub")),
        P(("mp", "sub"), None),
        P(),
    )
    return jax.shard_map(
        shards,
        mesh=mesh,
        in_specs=placed,
        out_specs=(P(("ens", "seq"), ("mp", "sub")), P(("ens", "seq"), ("mp", "sub"))),
        check_vma=False,
    )
```

```python
import functools

import jax
import jax.numpy as jnp
from jax import lax
from jax.experimental import pallas as pl
from jax.experimental.pallas import tpu as pltpu
from jax.sharding import PartitionSpec as P

HD = 64
WIN = 512
TILE = 128
ESIDE = 4
DSIDE = 4
STEP = 4
NEG = -1e30
BF = jnp.bfloat16
F32 = jnp.float32


def call(body, outs, args, flops, scratch=(), name=None, spare=8):
    moved = sum(a.size * a.dtype.itemsize for a in args)
    moved += sum(o.size * o.dtype.itemsize for o in outs)
    return pl.pallas_call(
        body,
        out_shape=tuple(outs),
        in_specs=[pl.BlockSpec(memory_space=pltpu.VMEM)] * len(args),
        out_specs=tuple(pl.BlockSpec(memory_space=pltpu.VMEM) for _ in outs),
        scratch_shapes=list(scratch),
        cost_estimate=pl.CostEstimate(flops=flops, bytes_accessed=moved, transcendentals=0),
        compiler_params=pltpu.CompilerParams(vmem_limit_bytes=moved + spare * 1024 * 1024),
        name=name,
    )(*args)


def column(row):
    return jnp.transpose(jnp.broadcast_to(row, (TILE, TILE)))


def picks(rows_ref, first, source_rows):
    cols = jnp.concatenate([column(rows_ref[pl.ds(first + i, 1), :]) for i in range(STEP)], axis=0)
    cols = cols.astype(jnp.int16)
    lane = lax.broadcasted_iota(jnp.int32, cols.shape, 1).astype(jnp.int16)
    tiles = []
    for j in range(source_rows // TILE):
        hit = cols == lane + jnp.int16(j * TILE)
        tiles.append(jnp.where(hit, jnp.ones_like(cols, BF), jnp.zeros_like(cols, BF)))
    return jnp.concatenate(tiles, axis=1)


def messages(src_ref, weight_ref, first, source_ref):
    picked = jnp.dot(
        picks(src_ref, first, source_ref.shape[0]), source_ref[...], preferred_element_type=F32
    )
    scale = jnp.concatenate([column(weight_ref[pl.ds(first + i, 1), :]) for i in range(STEP)], axis=0)
    scale = jnp.concatenate([scale] * (picked.shape[1] // TILE), axis=1)
    return (picked * scale).astype(BF)


def parity():
    return lax.rem(lax.axis_index("seq"), 2)


def outward(which, side):
    return jnp.where(parity() == which, side, 0)


def block_of(step, count):
    return step if count == 1 else jnp.where(parity() == 0, count - 1 - step, step)


def partners(count):
    first = [(i, i ^ 1) for i in range(count) if i ^ 1 < count]
    second = [(i, (i - 1 ^ 1) + 1) for i in range(1, count) if (i - 1 ^ 1) + 1 < count]
    return first, second


def put_messages(src_ref, weight_ref, first, source_ref, out, at):
    edges = STEP * TILE
    for k in range(out.shape[0] // edges):
        out[k * edges : (k + 1) * edges, :] = messages(
            src_ref, weight_ref, first + k * STEP, source_ref
        )


def side_body(side, src_ref, weight_ref, source_ref, first_ref, second_ref):
    for which, out in enumerate((first_ref, second_ref)):
        put_messages(src_ref, weight_ref, outward(which, side), source_ref, out, 0)


def gather_body(start, src_ref, weight_ref, source_ref, out_ref):
    edges = STEP * TILE
    pair = 2

    def step(k, carry):
        for i in range(pair):
            n = k * pair + i
            out_ref[pl.ds(pl.multiple_of(n * edges, edges), edges), :] = messages(
                src_ref, weight_ref, start + n * STEP, source_ref
            )
        return carry

    lax.fori_loop(0, out_ref.shape[0] // (pair * edges), step, 0)


def lands(rows_ref, tiles, base, target_rows):
    spot = lax.broadcasted_iota(jnp.int32, (target_rows, TILE), 0).astype(jnp.int16)
    out = []
    for tile in tiles:
        row = rows_ref[pl.ds(tile, 1), :] - base
        row = jnp.broadcast_to(row, (target_rows, TILE)).astype(jnp.int16)
        out.append(jnp.where(row == spot, jnp.ones_like(spot, BF), jnp.zeros_like(spot, BF)))
    return jnp.concatenate(out, axis=1)


def landed(side, dst_ref, first_ref, second_ref, local_ref, base, target_rows):
    first, second = outward(0, side), outward(1, side)
    n = local_ref.shape[0] // TILE
    total = jnp.dot(
        lands(dst_ref, [2 * side + i for i in range(n)], base, target_rows),
        local_ref[...],
        preferred_element_type=F32,
    )
    total = total + jnp.dot(
        lands(dst_ref, [first + i for i in range(side)], base, target_rows),
        first_ref[...],
        preferred_element_type=F32,
    )
    return total + jnp.dot(
        lands(dst_ref, [second + i for i in range(side)], base, target_rows),
        second_ref[...],
        preferred_element_type=F32,
    )


def latent_body(side, which, count, dst_ref, first_ref, second_ref, local_ref, embed_ref, out_ref):
    rows = out_ref.shape[0]
    base = block_of(which, count) * rows
    half = 256
    for h in range(rows // half):
        at = pl.multiple_of(base + h * half, half)
        got = landed(side, dst_ref, first_ref, second_ref, local_ref, at, half)
        out_ref[h * half : (h + 1) * half, :] = (
            embed_ref[pl.ds(at, half), :].astype(F32) + got
        ).astype(BF)


def grid_body(side, count_ref, dst_ref, first_ref, second_ref, local_ref, grid_ref, out_ref):
    half = 512

    def step(k, carry):
        for i in range(2):
            at = pl.multiple_of((2 * k + i) * half, half)
            got = landed(side, dst_ref, first_ref, second_ref, local_ref, at, half)
            row = at + lax.broadcasted_iota(jnp.int32, got.shape, 0)
            value = grid_ref[pl.ds(at, half), :].astype(F32) + got
            out_ref[pl.ds(at, half), :] = jnp.where(row < count_ref[0, 0], value, 0.0).astype(BF)
        return carry

    lax.fori_loop(0, out_ref.shape[0] // (2 * half), step, 0)


def swapped(first, second):
    one, two = partners(lax.axis_size("seq"))
    return lax.ppermute(first, "seq", one), lax.ppermute(second, "seq", two)


def gathered(edge_src, edge_weight, source, side):
    edges = edge_src.shape[0] * TILE - 2 * side * TILE
    out = jax.ShapeDtypeStruct((edges, source.shape[1]), BF)
    (local,) = call(
        functools.partial(gather_body, 2 * side),
        (out,),
        (edge_src, edge_weight, source),
        2 * edges * source.size,
        name="gather",
    )
    return local


def power(exponent):
    return jnp.where(exponent > 0, 2.0, jnp.where(exponent < 0, 0.5, 1.0)).astype(F32)


def place(step, parts):
    if parts == 1:
        return 0
    mp = lax.axis_index("mp")
    sub = lax.axis_index("sub")
    mp = mp if step < 2 else 1 - mp
    sub = sub if step % 2 == 0 else 1 - sub
    return 2 * mp + sub


def qkv_body(parts, *refs):
    pieces, (gain_ref, w_ref, normed_ref, q_ref, kv_ref) = refs[:parts], refs[parts:]
    rows, width = pieces[0].shape
    total = width * parts
    block = min(256, rows)
    lane = lax.broadcasted_iota(jnp.int32, (block, TILE), 1)

    def step(k, carry):
        at = pl.ds(pl.multiple_of(k * block, block), block)
        values = [p[at, :].astype(F32) for p in pieces]
        mean = sum(jnp.sum(v, axis=1, keepdims=True) for v in values) / total
        values = [v - mean for v in values]
        var = sum(jnp.sum(v * v, axis=1, keepdims=True) for v in values) / total
        scale = lax.rsqrt(var + 1e-05)
        for i, v in enumerate(values):
            cols = pl.ds(pl.multiple_of(place(i, parts) * width, width), width)
            normed_ref[at, cols] = (v * scale * gain_ref[:, cols]).astype(BF)
        out = jnp.dot(normed_ref[at, :], w_ref[...], preferred_element_type=F32)
        for pair in range(q_ref.shape[1] // TILE):
            a, b, c = [out[:, (3 * pair + i) * TILE : (3 * pair + i + 1) * TILE] for i in range(3)]
            q = pltpu.roll(jnp.where(lane < HD, a, b), HD, 1)
            q_ref[at, pair * TILE : (pair + 1) * TILE] = q.astype(BF)
            kv_ref[at, 2 * pair * TILE : (2 * pair + 1) * TILE] = jnp.where(lane < HD, b, a).astype(BF)
            kv_ref[at, (2 * pair + 1) * TILE : (2 * pair + 2) * TILE] = c.astype(BF)
        return carry

    lax.fori_loop(0, rows // block, step, 0)


def up_body(normed_ref, w_ref, exp_ref, out_ref):
    rows = normed_ref.shape[0]
    block = min(256, rows)
    cols = min(512, w_ref.shape[1])

    def step(k, carry):
        at = pl.ds(pl.multiple_of(k * block, block), block)
        for c in range(w_ref.shape[1] // cols):
            sl = slice(c * cols, (c + 1) * cols)
            up = jnp.dot(normed_ref[at, :], w_ref[:, sl], preferred_element_type=F32)
            up = up * power(exp_ref[:, sl])
            out_ref[at, sl] = (0.5 * up * (1.0 + lax.erf(up * 0.7071067811865476))).astype(BF)
        return carry

    lax.fori_loop(0, rows // block, step, 0)


def attend_body(which, q_ref, inner_ref, here_ref, outer_ref, out_ref):
    rows = q_ref.shape[0]
    block = 256
    n = WIN // block
    lane = lax.broadcasted_iota(jnp.int32, (block, TILE), 1)
    i = lax.broadcasted_iota(jnp.int32, (block, block), 0)
    j = lax.broadcasted_iota(jnp.int32, (block, block), 1)
    seq = lax.axis_index("seq")
    after = parity() == which
    outer_ok = jnp.where(after, seq < lax.axis_size("seq") - 1, seq > 0)
    outer_bias = jnp.where(outer_ok, 0.0, NEG).astype(F32)
    ahead = jnp.where(after, i - j, j - i)
    inner_mask = jnp.where(ahead <= 0, 0.0, NEG).astype(F32)
    outer_mask = jnp.where(ahead >= 0, outer_bias, NEG).astype(F32)
    contract = (((1,), (1,)), ((), ()))

    def at(b):
        return pl.ds(pl.multiple_of(jnp.where(after, b, n - 1 - b) * block, block), block)

    for pair in range(q_ref.shape[1] // TILE):
        pair_cols = slice(pair * TILE, (pair + 1) * TILE)
        for b in range(rows // block):
            q2 = q_ref[at(b), pair_cols]
            outs = []
            for half in range(2):
                cols = slice((2 * pair + half) * TILE, (2 * pair + half + 1) * TILE)
                keep = (lane >= HD) if half == 0 else (lane < HD)
                q = jnp.where(keep, q2 * BF(HD**-0.5), jnp.zeros_like(q2))
                keys = []
                for t in range(b, b + 2 * n + 1):
                    ref = (inner_ref, here_ref, outer_ref)[t // n]
                    keys.append((t, ref[at(t % n), cols]))
                scores = []
                for t, key in keys:
                    s = lax.dot_general(q, key, contract, preferred_element_type=F32)
                    if t == b:
                        s = s + inner_mask
                    elif t == b + 2 * n:
                        s = s + outer_mask
                    elif t >= 2 * n:
                        s = s + outer_bias
                    scores.append(s)
                peak = scores[0]
                for s in scores[1:]:
                    peak = jnp.maximum(peak, s)
                peak = jnp.max(peak, axis=1, keepdims=True)
                probs = [jnp.exp(s - peak) for s in scores]
                total = probs[0]
                for p in probs[1:]:
                    total = total + p
                total = jnp.sum(total, axis=1, keepdims=True)
                mixed = jnp.dot(
                    jnp.concatenate([p.astype(BF) for p in probs], axis=1),
                    jnp.concatenate([key for _, key in keys], axis=0),
                    preferred_element_type=F32,
                )
                outs.append(mixed / total)
            out_ref[at(b), pair_cols] = jnp.where(lane < HD, outs[0], outs[1]).astype(BF)


def down_body(parts, att_ref, act_ref, w_out_ref, w_down_ref, exp_ref, *outs):
    rows = att_ref.shape[0]
    width = w_out_ref.shape[1] // parts
    block = min(256, rows)

    def step(k, carry):
        at = pl.ds(pl.multiple_of(k * block, block), block)
        for i in range(parts):
            cols = pl.ds(pl.multiple_of(place(i, parts) * width, width), width)
            mlp = jnp.dot(act_ref[at, :], w_down_ref[:, cols], preferred_element_type=F32)
            att = jnp.dot(att_ref[at, :], w_out_ref[:, cols], preferred_element_type=F32)
            part = (att + mlp * power(exp_ref[:, cols])).astype(BF)
            outs[i][at, :] = part
        return carry

    lax.fori_loop(0, rows // block, step, 0)


SWAP = [(0, 1), (1, 0)]


def gather(rows, split):
    if not split:
        return [lax.all_gather(rows, ("mp", "sub"), axis=1, tiled=True)]
    far = lax.ppermute(rows, "mp", SWAP)
    near = lax.ppermute(rows, "sub", SWAP)
    both = lax.ppermute(far, "sub", SWAP)
    return [rows, near, far, both]


def reduce_parts(parts, split):
    if not split:
        return [lax.psum_scatter(parts[0], ("mp", "sub"), scatter_dimension=1, tiled=True)]
    own, near, far, both = parts
    far_got = lax.ppermute(both, "sub", SWAP)
    near_got = lax.ppermute(near, "sub", SWAP)
    far_sum = (far.astype(F32) + far_got.astype(F32)).astype(BF)
    return [own, near_got, lax.ppermute(far_sum, "mp", SWAP)]


def settle_body(side, count, terms, src_ref, weight_ref, *refs):
    adds, (hidden_ref, first_ref, second_ref) = refs[: count * terms], refs[count * terms :]
    rows = adds[0].shape[0]
    for c in range(count):
        at = pl.ds(pl.multiple_of(block_of(c, count) * rows, rows), rows)
        latent, *more = adds[c * terms : (c + 1) * terms]
        total = more[0][...].astype(F32)
        for term in more[1:]:
            total = total + term[...].astype(F32)
        hidden_ref[at, :] = (latent[...].astype(F32) + total).astype(BF)
    side_body(side, src_ref, weight_ref, hidden_ref, first_ref, second_ref)


def shards(
    grid_latent,
    grid_count,
    hidden_embed,
    enc_src_rows,
    enc_dst_rows,
    enc_weight,
    dec_src_rows,
    dec_dst_rows,
    dec_weight,
    norm_gain,
    w_qkv,
    w_out,
    w_up,
    up_exp,
    w_down,
    down_exp,
):
    split = lax.axis_size("mp") == 2 and lax.axis_size("sub") == 2
    parts = 4 if split else 1
    hid_rows, features = hidden_embed.shape
    full = w_qkv.shape[0]
    heads = w_qkv.shape[1] // (3 * HD)
    units = w_up.shape[1]
    rows = WIN
    count = hid_rows // rows
    assert count == 2
    src, dst, wts = enc_src_rows[0], enc_dst_rows[0], enc_weight[0]
    out = jax.ShapeDtypeStruct((ESIDE * TILE, features), BF)
    sides = call(
        functools.partial(side_body, ESIDE),
        (out, out),
        (src, wts, grid_latent),
        4 * ESIDE * TILE * grid_latent.size,
        name="side",
    )
    arrived = swapped(*sides)
    moved = gathered(src, wts, grid_latent, ESIDE)
    chunks = []
    for c in range(count):
        (part,) = call(
            functools.partial(latent_body, ESIDE, c, count),
            (jax.ShapeDtypeStruct((rows, features), BF),),
            (dst, *arrived, moved, hidden_embed),
            2 * dst.size * rows * features,
            name="latent",
        )
        chunks.append([part, gather(part, split)])
    for chunk in chunks:
        chunk.append(
            call(
                functools.partial(qkv_body, parts),
                (
                    jax.ShapeDtypeStruct((rows, full), BF),
                    jax.ShapeDtypeStruct((rows, heads * HD), BF),
                    jax.ShapeDtypeStruct((rows, 2 * heads * HD), BF),
                ),
                (*chunk[1], norm_gain[None, :], w_qkv),
                2 * rows * w_qkv.size,
                name="qkv",
            )
        )
    outer = swapped(chunks[0][2][2], chunks[1][2][2])
    for c, chunk in enumerate(chunks):
        part, _, (normed, q, kv) = chunk
        (activated,) = call(
            up_body,
            (jax.ShapeDtypeStruct((rows, units), BF),),
            (normed, w_up, up_exp[None, :]),
            2 * rows * w_up.size,
            name="up",
        )
        (attended,) = call(
            functools.partial(attend_body, c),
            (jax.ShapeDtypeStruct((rows, heads * HD), BF),),
            (q, chunks[1 - c][2][2], kv, outer[c]),
            4 * rows * 3 * WIN * heads * HD,
            name="attend",
            spare=12,
        )
        outs = call(
            functools.partial(down_body, parts),
            [jax.ShapeDtypeStruct((rows, full // parts), BF)] * parts,
            (attended, activated, w_out, w_down, down_exp[None, :]),
            2 * rows * (w_out.size + w_down.size),
            name="down",
        )
        chunk.append([part, *reduce_parts(outs, split)])
    adds = [term for chunk in chunks for term in chunk[3]]
    src, dst, wts = dec_src_rows[0], dec_dst_rows[0], dec_weight[0]
    out = jax.ShapeDtypeStruct((DSIDE * TILE, features), BF)
    hidden_out, *sides = call(
        functools.partial(settle_body, DSIDE, count, len(adds) // count),
        (jax.ShapeDtypeStruct(hidden_embed.shape, BF), out, out),
        (src, wts, *adds),
        4 * DSIDE * TILE * hidden_embed.size,
        name="settle",
    )
    arrived = swapped(*sides)
    moved = gathered(src, wts, hidden_out, DSIDE)
    (grid_out,) = call(
        functools.partial(grid_body, DSIDE),
        (jax.ShapeDtypeStruct(grid_latent.shape, BF),),
        (grid_count[None, :], dst, *arrived, moved, grid_latent),
        2 * dst.size * grid_latent.size,
        name="grid",
    )
    return (hidden_out, grid_out)


def solution(mesh):
    placed = (
        P(("ens", "seq"), ("mp", "sub")),
        P(("ens", "seq")),
        P(("ens", "seq"), ("mp", "sub")),
        P(("ens", "seq"), None, None),
        P(("ens", "seq"), None, None),
        P(("ens", "seq"), None, None),
        P(("ens", "seq"), None, None),
        P(("ens", "seq"), None, None),
        P(("ens", "seq"), None, None),
        P(),
        P(None, ("mp", "sub")),
        P(("mp", "sub"), None),
        P(None, ("mp", "sub")),
        P(("mp", "sub")),
        P(("mp", "sub"), None),
        P(),
    )
    return jax.shard_map(
        shards,
        mesh=mesh,
        in_specs=placed,
        out_specs=(P(("ens", "seq"), ("mp", "sub")), P(("ens", "seq"), ("mp", "sub"))),
        check_vma=False,
    )
```

```python
import functools

import jax
import jax.numpy as jnp
from jax import lax
from jax.experimental import pallas as pl
from jax.experimental.pallas import tpu as pltpu
from jax.sharding import PartitionSpec as P

HD = 64
WIN = 512
TILE = 128
ESIDE = 4
DSIDE = 4
STEP = 4
BLOCK = 256
NEG = -1e30
BF = jnp.bfloat16
F32 = jnp.float32


def call(body, outs, args, flops, scratch=(), spare=8, space=pltpu.VMEM, limit=None):
    moved = sum(a.size * a.dtype.itemsize for a in args)
    moved += sum(o.size * o.dtype.itemsize for o in outs)
    return pl.pallas_call(
        body,
        out_shape=tuple(outs),
        in_specs=[pl.BlockSpec(memory_space=space)] * len(args),
        out_specs=tuple(pl.BlockSpec(memory_space=pltpu.VMEM) for _ in outs),
        scratch_shapes=list(scratch),
        cost_estimate=pl.CostEstimate(flops=flops, bytes_accessed=moved, transcendentals=0),
        compiler_params=pltpu.CompilerParams(vmem_limit_bytes=limit or moved + spare * 1024 * 1024),
    )(*args)


def column(row):
    return jnp.transpose(jnp.broadcast_to(row, (TILE, TILE)))


def picks(rows_ref, first, source_rows):
    cols = jnp.concatenate([column(rows_ref[pl.ds(first + i, 1), :]) for i in range(STEP)], axis=0)
    cols = cols.astype(jnp.int16)
    lane = lax.broadcasted_iota(jnp.int32, cols.shape, 1).astype(jnp.int16)
    tiles = []
    for j in range(source_rows // TILE):
        hit = cols == lane + jnp.int16(j * TILE)
        tiles.append(jnp.where(hit, jnp.ones_like(cols, BF), jnp.zeros_like(cols, BF)))
    return jnp.concatenate(tiles, axis=1)


def messages(src_ref, weight_ref, first, source_ref):
    picked = jnp.dot(
        picks(src_ref, first, source_ref.shape[0]), source_ref[...], preferred_element_type=F32
    )
    scale = jnp.concatenate([column(weight_ref[pl.ds(first + i, 1), :]) for i in range(STEP)], axis=0)
    scale = jnp.concatenate([scale] * (picked.shape[1] // TILE), axis=1)
    return (picked * scale).astype(BF)


def parity():
    return lax.rem(lax.axis_index("seq"), 2)


def outward(which, side):
    return jnp.where(parity() == which, side, 0)


def block_of(step, count):
    return step if count == 1 else jnp.where(parity() == 0, count - 1 - step, step)


def partners(count):
    first = [(i, i ^ 1) for i in range(count) if i ^ 1 < count]
    second = [(i, (i - 1 ^ 1) + 1) for i in range(1, count) if (i - 1 ^ 1) + 1 < count]
    return first, second


def put_messages(src_ref, weight_ref, first, source_ref, out):
    edges = STEP * TILE
    for k in range(out.shape[0] // edges):
        out[k * edges : (k + 1) * edges, :] = messages(
            src_ref, weight_ref, first + k * STEP, source_ref
        )


def side_body(side, src_ref, weight_ref, source_ref, first_ref, second_ref):
    for which, out in enumerate((first_ref, second_ref)):
        put_messages(src_ref, weight_ref, outward(which, side), source_ref, out)


def fetch_side_body(side, *refs):
    sources, outs, held, sems = refs[:3], refs[3:5], refs[5:8], refs[8]
    copies = [pltpu.make_async_copy(a, b, sems.at[i]) for i, (a, b) in enumerate(zip(sources, held))]
    for copy in copies:
        copy.start()
    for copy in copies:
        copy.wait()
    side_body(side, *held, *outs)


def gather_body(start, src_ref, weight_ref, source_ref, out_ref):
    edges = STEP * TILE
    pair = 2

    def step(k, carry):
        for i in range(pair):
            n = k * pair + i
            out_ref[pl.ds(pl.multiple_of(n * edges, edges), edges), :] = messages(
                src_ref, weight_ref, start + n * STEP, source_ref
            )
        return carry

    lax.fori_loop(0, out_ref.shape[0] // (pair * edges), step, 0)


def lands(rows_ref, tiles, base, target_rows):
    spot = lax.broadcasted_iota(jnp.int32, (target_rows, TILE), 0).astype(jnp.int16)
    out = []
    for tile in tiles:
        row = rows_ref[pl.ds(tile, 1), :] - base
        row = jnp.broadcast_to(row, (target_rows, TILE)).astype(jnp.int16)
        out.append(jnp.where(row == spot, jnp.ones_like(spot, BF), jnp.zeros_like(spot, BF)))
    return jnp.concatenate(out, axis=1)


def landed(side, dst_ref, first_ref, second_ref, base, target_rows):
    total = None
    for which, got_ref in enumerate((first_ref, second_ref)):
        first = outward(which, side)
        got = jnp.dot(
            lands(dst_ref, [first + i for i in range(side)], base, target_rows),
            got_ref[...],
            preferred_element_type=F32,
        )
        total = got if total is None else total + got
    return total


def spread_body(side, dst_ref, local_ref, out_ref):
    block = 512

    def step(k, carry):
        for i in range(2):
            at = pl.multiple_of((2 * k + i) * block, block)
            tiles = [2 * side + t for t in range(local_ref.shape[0] // TILE)]
            out_ref[pl.ds(at, block), :] = jnp.dot(
                lands(dst_ref, tiles, at, block), local_ref[...], preferred_element_type=F32
            )
        return carry

    lax.fori_loop(0, out_ref.shape[0] // (2 * block), step, 0)


def latent_body(side, which, count, dst_ref, first_ref, second_ref, total_ref, embed_ref, out_ref):
    rows = out_ref.shape[0]
    base = block_of(which, count) * rows
    for h in range(rows // BLOCK):
        at = pl.multiple_of(base + h * BLOCK, BLOCK)
        got = landed(side, dst_ref, first_ref, second_ref, at, BLOCK)
        got = got + total_ref[pl.ds(at, BLOCK), :]
        out_ref[h * BLOCK : (h + 1) * BLOCK, :] = (
            embed_ref[pl.ds(at, BLOCK), :].astype(F32) + got
        ).astype(BF)


def grid_body(side, count_ref, dst_ref, first_ref, second_ref, total_ref, grid_ref, out_ref):
    rows = out_ref.shape[0]
    for h in range(rows // BLOCK):
        at = pl.program_id(0) * rows + h * BLOCK
        here = slice(h * BLOCK, (h + 1) * BLOCK)
        got = landed(side, dst_ref, first_ref, second_ref, at, BLOCK) + total_ref[here, :]
        row = at + lax.broadcasted_iota(jnp.int32, got.shape, 0)
        value = grid_ref[here, :].astype(F32) + got
        out_ref[here, :] = jnp.where(row < count_ref[0, 0], value, 0.0).astype(BF)


def swapped(first, second):
    one, two = partners(lax.axis_size("seq"))
    return lax.ppermute(first, "seq", one), lax.ppermute(second, "seq", two)


def gathered(edge_src, edge_dst, edge_weight, source, target_rows, side):
    edges = edge_src.shape[0] * TILE - 2 * side * TILE
    features = source.shape[1]
    (local,) = call(
        functools.partial(gather_body, 2 * side),
        (jax.ShapeDtypeStruct((edges, features), BF),),
        (edge_src, edge_weight, source),
        2 * edges * source.size,
    )
    (total,) = call(
        functools.partial(spread_body, side),
        (jax.ShapeDtypeStruct((target_rows, features), F32),),
        (edge_dst, local),
        2 * edges * target_rows * features,
    )
    return total


def settled(side, grid_count, edge_dst, first, second, total, grid_latent):
    rows, features = grid_latent.shape
    block = 512
    whole = pl.BlockSpec(memory_space=pltpu.VMEM)
    piece = pl.BlockSpec((block, features), lambda i: (i, 0))
    return pl.pallas_call(
        functools.partial(grid_body, side),
        grid=(rows // block,),
        out_shape=jax.ShapeDtypeStruct(grid_latent.shape, BF),
        in_specs=[whole, whole, whole, whole, piece, piece],
        out_specs=piece,
        cost_estimate=pl.CostEstimate(
            flops=4 * side * TILE * grid_latent.size,
            bytes_accessed=8 * grid_latent.size,
            transcendentals=0,
        ),
        compiler_params=pltpu.CompilerParams(vmem_limit_bytes=16 * 1024 * 1024),
        name="grid",
    )(grid_count, edge_dst, first, second, total, grid_latent)


def power(exponent):
    return jnp.where(exponent > 0, 2.0, jnp.where(exponent < 0, 0.5, 1.0)).astype(F32)


def place(step, parts):
    if parts == 1:
        return 0
    mp = lax.axis_index("mp")
    sub = lax.axis_index("sub")
    mp = mp if step < 2 else 1 - mp
    sub = sub if step % 2 == 0 else 1 - sub
    return 2 * mp + sub


def qkv_body(parts, *refs):
    pieces, (gain_ref, w_ref, normed_ref, q_ref, kv_ref) = refs[:parts], refs[parts:]
    rows, width = pieces[0].shape
    total = width * parts
    block = min(256, rows)
    lane = lax.broadcasted_iota(jnp.int32, (block, TILE), 1)

    def step(k, carry):
        at = pl.ds(pl.multiple_of(k * block, block), block)
        values = [p[at, :].astype(F32) for p in pieces]
        mean = sum(jnp.sum(v, axis=1, keepdims=True) for v in values) / total
        values = [v - mean for v in values]
        var = sum(jnp.sum(v * v, axis=1, keepdims=True) for v in values) / total
        scale = lax.rsqrt(var + 1e-05)
        for i, v in enumerate(values):
            cols = pl.ds(pl.multiple_of(place(i, parts) * width, width), width)
            normed_ref[at, cols] = (v * scale * gain_ref[:, cols]).astype(BF)
        out = jnp.dot(normed_ref[at, :], w_ref[...], preferred_element_type=F32)
        for pair in range(q_ref.shape[1] // TILE):
            a, b, c = [out[:, (3 * pair + i) * TILE : (3 * pair + i + 1) * TILE] for i in range(3)]
            q = pltpu.roll(jnp.where(lane < HD, a, b), HD, 1)
            q_ref[at, pair * TILE : (pair + 1) * TILE] = q.astype(BF)
            kv_ref[at, 2 * pair * TILE : (2 * pair + 1) * TILE] = jnp.where(lane < HD, b, a).astype(BF)
            kv_ref[at, (2 * pair + 1) * TILE : (2 * pair + 2) * TILE] = c.astype(BF)
        return carry

    lax.fori_loop(0, rows // block, step, 0)


def up_body(normed_ref, w_ref, exp_ref, out_ref):
    rows = normed_ref.shape[0]
    block = min(256, rows)
    cols = min(512, w_ref.shape[1])

    def step(k, carry):
        at = pl.ds(pl.multiple_of(k * block, block), block)
        for c in range(w_ref.shape[1] // cols):
            sl = slice(c * cols, (c + 1) * cols)
            up = jnp.dot(normed_ref[at, :], w_ref[:, sl], preferred_element_type=F32)
            up = up * power(exp_ref[:, sl])
            out_ref[at, sl] = (0.5 * up * (1.0 + lax.erf(up * 0.7071067811865476))).astype(BF)
        return carry

    lax.fori_loop(0, rows // block, step, 0)


def spot(which, b):
    n = WIN // BLOCK
    where = jnp.where(parity() == which, b, n - 1 - b)
    return pl.ds(pl.multiple_of(where * BLOCK, BLOCK), BLOCK)


def attend_body(which, blocks, q_ref, inner_ref, here_ref, outer_ref, out_ref):
    block = BLOCK
    n = WIN // block
    lane = lax.broadcasted_iota(jnp.int32, (block, TILE), 1)
    i = lax.broadcasted_iota(jnp.int32, (block, block), 0)
    j = lax.broadcasted_iota(jnp.int32, (block, block), 1)
    seq = lax.axis_index("seq")
    after = parity() == which
    outer_ok = jnp.where(after, seq < lax.axis_size("seq") - 1, seq > 0)
    outer_bias = jnp.where(outer_ok, 0.0, NEG).astype(F32)
    ahead = jnp.where(after, i - j, j - i)
    inner_mask = jnp.where(ahead <= 0, 0.0, NEG).astype(F32)
    outer_mask = jnp.where(ahead >= 0, outer_bias, NEG).astype(F32)
    contract = (((1,), (1,)), ((), ()))

    for pair in range(q_ref.shape[1] // TILE):
        pair_cols = slice(pair * TILE, (pair + 1) * TILE)
        for k, b in enumerate(blocks):
            q2 = q_ref[spot(which, b), pair_cols]
            outs = []
            for half in range(2):
                cols = slice((2 * pair + half) * TILE, (2 * pair + half + 1) * TILE)
                keep = (lane >= HD) if half == 0 else (lane < HD)
                q = jnp.where(keep, q2 * BF(HD**-0.5), jnp.zeros_like(q2))
                keys = []
                for t in range(b, b + 2 * n + 1):
                    ref = (inner_ref, here_ref, outer_ref)[t // n]
                    keys.append((t, ref[spot(which, t % n), cols]))
                scores = []
                for t, key in keys:
                    s = lax.dot_general(q, key, contract, preferred_element_type=F32)
                    if t == b:
                        s = s + inner_mask
                    elif t == b + 2 * n:
                        s = s + outer_mask
                    elif t >= 2 * n:
                        s = s + outer_bias
                    scores.append(s)
                peak = scores[0]
                for s in scores[1:]:
                    peak = jnp.maximum(peak, s)
                peak = jnp.max(peak, axis=1, keepdims=True)
                probs = [jnp.exp(s - peak) for s in scores]
                total = probs[0]
                for p in probs[1:]:
                    total = total + p
                total = jnp.sum(total, axis=1, keepdims=True)
                mixed = jnp.dot(
                    jnp.concatenate([p.astype(BF) for p in probs], axis=1),
                    jnp.concatenate([key for _, key in keys], axis=0),
                    preferred_element_type=F32,
                )
                outs.append(mixed / total)
            out_ref[k * block : (k + 1) * block, pair_cols] = jnp.where(
                lane < HD, outs[0], outs[1]
            ).astype(BF)


def down_body(parts, which, blocks, att_ref, act_ref, w_out_ref, w_down_ref, exp_ref, *outs):
    width = w_out_ref.shape[1] // parts
    for k, b in enumerate(blocks):
        at = slice(k * BLOCK, (k + 1) * BLOCK)
        for i in range(parts):
            cols = pl.ds(pl.multiple_of(place(i, parts) * width, width), width)
            mlp = jnp.dot(act_ref[spot(which, b), :], w_down_ref[:, cols], preferred_element_type=F32)
            att = jnp.dot(att_ref[at, :], w_out_ref[:, cols], preferred_element_type=F32)
            outs[i][at, :] = (att + mlp * power(exp_ref[:, cols])).astype(BF)


SWAP = [(0, 1), (1, 0)]
UNITS = ((0, (0, 1)), (1, (0,)), (1, (1,)))


def gather(rows, split):
    if not split:
        return [lax.all_gather(rows, ("mp", "sub"), axis=1, tiled=True)]
    far = lax.ppermute(rows, "mp", SWAP)
    near = lax.ppermute(rows, "sub", SWAP)
    both = lax.ppermute(far, "sub", SWAP)
    return [rows, near, far, both]


def reduce_parts(parts, split):
    if not split:
        return [lax.psum_scatter(parts[0], ("mp", "sub"), scatter_dimension=1, tiled=True)]
    own, near, far, both = parts
    far_got = lax.ppermute(both, "sub", SWAP)
    near_got = lax.ppermute(near, "sub", SWAP)
    far_sum = (far.astype(F32) + far_got.astype(F32)).astype(BF)
    return [own, near_got, lax.ppermute(far_sum, "mp", SWAP)]


def settle_body(side, count, units, src_ref, weight_ref, *refs):
    latents, refs = refs[:count], refs[count:]
    terms = (len(refs) - 4) // len(units)
    hidden_ref, copy_ref, first_ref, second_ref = refs[-4:]
    for u, (c, blocks) in enumerate(units):
        adds = refs[u * terms : (u + 1) * terms]
        base = block_of(c, count) * WIN
        for k, b in enumerate(blocks):
            at = slice(k * BLOCK, (k + 1) * BLOCK)
            total = adds[0][at, :].astype(F32)
            for term in adds[1:]:
                total = total + term[at, :].astype(F32)
            spots = spot(c, b)
            value = (latents[c][spots, :].astype(F32) + total).astype(BF)
            rows = pl.ds(pl.multiple_of(base + spots.start, BLOCK), BLOCK)
            hidden_ref[rows, :] = value
            copy_ref[rows, :] = value
    side_body(side, src_ref, weight_ref, copy_ref, first_ref, second_ref)


def shards(
    grid_latent,
    grid_count,
    hidden_embed,
    enc_src_rows,
    enc_dst_rows,
    enc_weight,
    dec_src_rows,
    dec_dst_rows,
    dec_weight,
    norm_gain,
    w_qkv,
    w_out,
    w_up,
    up_exp,
    w_down,
    down_exp,
):
    split = lax.axis_size("mp") == 2 and lax.axis_size("sub") == 2
    parts = 4 if split else 1
    hid_rows, features = hidden_embed.shape
    full = w_qkv.shape[0]
    heads = w_qkv.shape[1] // (3 * HD)
    units = w_up.shape[1]
    rows = WIN
    count = hid_rows // rows
    assert count == 2
    src, dst, wts = enc_src_rows[0], enc_dst_rows[0], enc_weight[0]
    out = jax.ShapeDtypeStruct((ESIDE * TILE, features), BF)
    args = (src, wts, grid_latent)
    sides = call(
        functools.partial(fetch_side_body, ESIDE),
        (out, out),
        args,
        4 * ESIDE * TILE * grid_latent.size,
        scratch=[
            *(pltpu.VMEM(a.shape, a.dtype) for a in args),
            pltpu.SemaphoreType.DMA((len(args),)),
        ],
        space=pltpu.HBM,
        limit=60 * 1024 * 1024,
    )
    arrived = swapped(*sides)
    total = gathered(src, dst, wts, grid_latent, hid_rows, ESIDE)
    chunks = []
    for c in range(count):
        (part,) = call(
            functools.partial(latent_body, ESIDE, c, count),
            (jax.ShapeDtypeStruct((rows, features), BF),),
            (dst, *arrived, total, hidden_embed),
            4 * ESIDE * TILE * rows * features,
        )
        chunks.append([part, gather(part, split)])
    for chunk in chunks:
        chunk.append(
            call(
                functools.partial(qkv_body, parts),
                (
                    jax.ShapeDtypeStruct((rows, full), BF),
                    jax.ShapeDtypeStruct((rows, heads * HD), BF),
                    jax.ShapeDtypeStruct((rows, 2 * heads * HD), BF),
                ),
                (*chunk[1], norm_gain[None, :], w_qkv),
                2 * rows * w_qkv.size,
            )
        )
    outer = swapped(chunks[0][2][2], chunks[1][2][2])
    for chunk in chunks:
        (activated,) = call(
            up_body,
            (jax.ShapeDtypeStruct((rows, units), BF),),
            (chunk[2][0], w_up, up_exp[None, :]),
            2 * rows * w_up.size,
        )
        chunk.append(activated)
    sums = []
    for c, blocks in UNITS:
        part, _, (_, q, kv), activated = chunks[c]
        size = len(blocks) * BLOCK
        (attended,) = call(
            functools.partial(attend_body, c, blocks),
            (jax.ShapeDtypeStruct((size, heads * HD), BF),),
            (q, chunks[1 - c][2][2], kv, outer[c]),
            4 * size * 3 * WIN * heads * HD,
            spare=12,
        )
        outs = call(
            functools.partial(down_body, parts, c, blocks),
            [jax.ShapeDtypeStruct((size, full // parts), BF)] * parts,
            (attended, activated, w_out, w_down, down_exp[None, :]),
            2 * size * (w_out.size + w_down.size),
        )
        sums += reduce_parts(outs, split)
    src, dst, wts = dec_src_rows[0], dec_dst_rows[0], dec_weight[0]
    out = jax.ShapeDtypeStruct((DSIDE * TILE, features), BF)
    whole = jax.ShapeDtypeStruct(hidden_embed.shape, BF)
    hidden_out, hidden, *sides = call(
        functools.partial(settle_body, DSIDE, count, UNITS),
        (whole, whole, out, out),
        (src, wts, *(chunk[0] for chunk in chunks), *sums),
        4 * DSIDE * TILE * hidden_embed.size,
    )
    arrived = swapped(*sides)
    total = gathered(src, dst, wts, hidden, grid_latent.shape[0], DSIDE)
    grid_out = settled(DSIDE, grid_count[None, :], dst, *arrived, total, grid_latent)
    return (hidden_out, grid_out)


def solution(mesh):
    placed = (
        P(("ens", "seq"), ("mp", "sub")),
        P(("ens", "seq")),
        P(("ens", "seq"), ("mp", "sub")),
        P(("ens", "seq"), None, None),
        P(("ens", "seq"), None, None),
        P(("ens", "seq"), None, None),
        P(("ens", "seq"), None, None),
        P(("ens", "seq"), None, None),
        P(("ens", "seq"), None, None),
        P(),
        P(None, ("mp", "sub")),
        P(("mp", "sub"), None),
        P(None, ("mp", "sub")),
        P(("mp", "sub")),
        P(("mp", "sub"), None),
        P(),
    )
    return jax.shard_map(
        shards,
        mesh=mesh,
        in_specs=placed,
        out_specs=(P(("ens", "seq"), ("mp", "sub")), P(("ens", "seq"), ("mp", "sub"))),
        check_vma=False,
    )
```

```python
import functools

import jax
import jax.numpy as jnp
from jax import lax
from jax.experimental import pallas as pl
from jax.experimental.pallas import tpu as pltpu
from jax.sharding import PartitionSpec as P

HD = 64
WIN = 512
TILE = 128
ESIDE = 4
DSIDE = 4
STEP = 4
BLOCK = 256
NEG = -1e30
BF = jnp.bfloat16
F32 = jnp.float32


def call(body, outs, args, flops, scratch=(), spare=8, space=pltpu.VMEM, limit=None):
    moved = sum(a.size * a.dtype.itemsize for a in args)
    moved += sum(o.size * o.dtype.itemsize for o in outs)
    return pl.pallas_call(
        body,
        out_shape=tuple(outs),
        in_specs=[pl.BlockSpec(memory_space=space)] * len(args),
        out_specs=tuple(pl.BlockSpec(memory_space=pltpu.VMEM) for _ in outs),
        scratch_shapes=list(scratch),
        cost_estimate=pl.CostEstimate(flops=flops, bytes_accessed=moved, transcendentals=0),
        compiler_params=pltpu.CompilerParams(vmem_limit_bytes=limit or moved + spare * 1024 * 1024),
    )(*args)


def column(row):
    return jnp.transpose(jnp.broadcast_to(row, (TILE, TILE)))


def picks(rows_ref, first, base, source_rows):
    tiles = [column(rows_ref[pl.ds(first + i, 1), :] - base) for i in range(STEP)]
    cols = jnp.concatenate(tiles, axis=0)
    cols = cols.astype(jnp.int16)
    lane = lax.broadcasted_iota(jnp.int32, cols.shape, 1).astype(jnp.int16)
    tiles = []
    for j in range(source_rows // TILE):
        hit = cols == lane + jnp.int16(j * TILE)
        tiles.append(jnp.where(hit, jnp.ones_like(cols, BF), jnp.zeros_like(cols, BF)))
    return jnp.concatenate(tiles, axis=1)


def picked(src_ref, first, sources, bases):
    total = None
    for source_ref, base in zip(sources, bases):
        part = jnp.dot(
            picks(src_ref, first, base, source_ref.shape[0]),
            source_ref[...],
            preferred_element_type=F32,
        )
        total = part if total is None else total + part
    return total


def scaled(rows, weight_ref, first):
    scale = jnp.concatenate([column(weight_ref[pl.ds(first + i, 1), :]) for i in range(STEP)], axis=0)
    return (rows * jnp.concatenate([scale] * (rows.shape[1] // TILE), axis=1)).astype(BF)


def parity():
    return lax.rem(lax.axis_index("seq"), 2)


def outward(which, side):
    return jnp.where(parity() == which, side, 0)


def block_of(step, count):
    return step if count == 1 else jnp.where(parity() == 0, count - 1 - step, step)


def partners(count, groups):
    both = []
    for which in range(2):
        pairs = []
        for e in range(groups):
            for i in range(count):
                j = ((i - which) ^ 1) + which
                if 0 <= j < count:
                    pairs.append((e * count + i, e * count + j))
                elif e ^ 1 < groups:
                    pairs.append((e * count + i, (e ^ 1) * count + i))
        both.append(pairs)
    return both


def has_partner(which):
    seq = lax.axis_index("seq")
    return jnp.where(parity() == which, seq < lax.axis_size("seq") - 1, seq > 0)


def sides(side, src_ref, weight_ref, sources, bases, outs, before=None):
    edges = STEP * TILE
    for which, out in enumerate(outs):
        for k in range(out.shape[0] // edges):
            at = slice(k * edges, (k + 1) * edges)
            first = outward(which, side) + k * STEP
            rows = picked(src_ref, first, sources, bases)
            if before is not None:
                rows = rows + before[which][at, :].astype(F32)
            out[at, :] = rows.astype(BF) if weight_ref is None else scaled(rows, weight_ref, first)


def fetch_side_body(side, *refs):
    sources, outs, held, sems = refs[:3], refs[3:5], refs[5:8], refs[8]
    copies = [pltpu.make_async_copy(a, b, sems.at[i]) for i, (a, b) in enumerate(zip(sources, held))]
    for copy in copies:
        copy.start()
    for copy in copies:
        copy.wait()
    sides(side, held[0], held[1], held[2:], (0,), outs)


def locals_(start, src_ref, weight_ref, sources, bases, out_ref, before_ref=None):
    edges = STEP * TILE
    pair = 2

    def step(k, carry):
        for i in range(pair):
            n = k * pair + i
            at = pl.ds(pl.multiple_of(n * edges, edges), edges)
            first = start + n * STEP
            rows = picked(src_ref, first, sources, bases)
            if before_ref is not None:
                rows = rows + before_ref[at, :].astype(F32)
            out_ref[at, :] = rows.astype(BF) if weight_ref is None else scaled(rows, weight_ref, first)
        return carry

    lax.fori_loop(0, out_ref.shape[0] // (pair * edges), step, 0)


def gather_body(start, src_ref, weight_ref, source_ref, out_ref):
    locals_(start, src_ref, weight_ref, (source_ref,), (0,), out_ref)


def lands(rows_ref, tiles, base, target_rows, there=None):
    spot = lax.broadcasted_iota(jnp.int32, (target_rows, TILE), 0).astype(jnp.int16)
    out = []
    for tile in tiles:
        row = rows_ref[pl.ds(tile, 1), :] - base
        row = row if there is None else jnp.where(there, row, -1)
        row = jnp.broadcast_to(row, (target_rows, TILE)).astype(jnp.int16)
        out.append(jnp.where(row == spot, jnp.ones_like(spot, BF), jnp.zeros_like(spot, BF)))
    return jnp.concatenate(out, axis=1)


def landed(side, dst_ref, first_ref, second_ref, base, target_rows):
    total = None
    for which, got_ref in enumerate((first_ref, second_ref)):
        first = outward(which, side)
        got = jnp.dot(
            lands(dst_ref, [first + i for i in range(side)], base, target_rows, has_partner(which)),
            got_ref[...],
            preferred_element_type=F32,
        )
        total = got if total is None else total + got
    return total


def spread_body(side, dst_ref, local_ref, out_ref):
    block = 512

    def step(k, carry):
        for i in range(2):
            at = pl.multiple_of((2 * k + i) * block, block)
            tiles = [2 * side + t for t in range(local_ref.shape[0] // TILE)]
            out_ref[pl.ds(at, block), :] = jnp.dot(
                lands(dst_ref, tiles, at, block), local_ref[...], preferred_element_type=F32
            )
        return carry

    lax.fori_loop(0, out_ref.shape[0] // (2 * block), step, 0)


def start_of(c, b, count):
    return block_of(c, count) * WIN + spot(c, b)


def latent_body(side, c, b, count, dst_ref, first_ref, second_ref, total_ref, embed_ref, out_ref):
    at = pl.multiple_of(start_of(c, b, count), BLOCK)
    got = landed(side, dst_ref, first_ref, second_ref, at, BLOCK)
    got = got + total_ref[pl.ds(at, BLOCK), :]
    out_ref[...] = (embed_ref[pl.ds(at, BLOCK), :].astype(F32) + got).astype(BF)


def grid_body(side, count, count_ref, dst_ref, first_ref, second_ref, total_ref, grid_ref, *refs):
    *hiddens, hidden_ref, out_ref = refs
    rows = out_ref.shape[0]
    step = pl.program_id(0)
    for h in range(rows // BLOCK):
        at = pl.multiple_of(step * rows + h * BLOCK, BLOCK)
        here = slice(h * BLOCK, (h + 1) * BLOCK)
        from_ = pl.ds(at, BLOCK)
        got = landed(side, dst_ref, first_ref, second_ref, at, BLOCK) + total_ref[from_, :]
        row = at + lax.broadcasted_iota(jnp.int32, got.shape, 0)
        value = grid_ref[from_, :].astype(F32) + got
        out_ref[here, :] = jnp.where(row < count_ref[0, 0], value, 0.0).astype(BF)
    for unit, unit_ref in zip(UNITS, hiddens):
        for k, start in enumerate(unit_starts(unit, count)):

            @pl.when(start == step * BLOCK)
            def _():
                hidden_ref[...] = unit_ref[k * BLOCK : (k + 1) * BLOCK, :]


def swapped(first, second):
    one, two = partners(lax.axis_size("seq"), lax.axis_size("ens"))
    axes = ("ens", "seq")
    return lax.ppermute(first, axes, one), lax.ppermute(second, axes, two)


def gathered(edge_src, edge_weight, source, side):
    edges = edge_src.shape[0] * TILE - 2 * side * TILE
    (local,) = call(
        functools.partial(gather_body, 2 * side),
        (jax.ShapeDtypeStruct((edges, source.shape[1]), BF),),
        (edge_src, edge_weight, source),
        2 * edges * source.size,
    )
    return local


def spread(edge_dst, local, target_rows, side):
    (total,) = call(
        functools.partial(spread_body, side),
        (jax.ShapeDtypeStruct((target_rows, local.shape[1]), F32),),
        (edge_dst, local),
        2 * local.size * target_rows,
    )
    return total


def settled(side, count, grid_count, edge_dst, first, second, total, grid_latent, hiddens):
    rows, features = grid_latent.shape
    steps = sum(h.shape[0] for h in hiddens) // BLOCK
    block = rows // steps
    args = (grid_count, edge_dst, first, second, total, grid_latent, *hiddens)
    return pl.pallas_call(
        functools.partial(grid_body, side, count),
        grid=(steps,),
        out_shape=(
            jax.ShapeDtypeStruct((steps * BLOCK, features), BF),
            jax.ShapeDtypeStruct((rows, features), BF),
        ),
        in_specs=[pl.BlockSpec(memory_space=pltpu.VMEM)] * len(args),
        out_specs=(
            pl.BlockSpec((BLOCK, features), lambda i: (i, 0)),
            pl.BlockSpec((block, features), lambda i: (i, 0)),
        ),
        cost_estimate=pl.CostEstimate(
            flops=4 * side * TILE * grid_latent.size,
            bytes_accessed=8 * grid_latent.size,
            transcendentals=0,
        ),
        compiler_params=pltpu.CompilerParams(vmem_limit_bytes=16 * 1024 * 1024),
        name="grid",
    )(*args)


def power(exponent):
    return jnp.where(exponent > 0, 2.0, jnp.where(exponent < 0, 0.5, 1.0)).astype(F32)


def place(step, parts):
    if parts == 1:
        return 0
    mp = lax.axis_index("mp")
    sub = lax.axis_index("sub")
    mp = mp if step < 2 else 1 - mp
    sub = sub if step % 2 == 0 else 1 - sub
    return 2 * mp + sub


def qkv_body(parts, *refs):
    pieces, (gain_ref, w_ref, *refs) = refs[:parts], refs[parts:]
    normed_ref, q_ref, kv_ref = refs
    rows, width = pieces[0].shape
    total = width * parts
    block = min(256, rows)
    lane = lax.broadcasted_iota(jnp.int32, (block, TILE), 1)

    def step(k, carry):
        at = pl.ds(pl.multiple_of(k * block, block), block)
        values = [p[at, :].astype(F32) for p in pieces]
        mean = sum(jnp.sum(v, axis=1, keepdims=True) for v in values) / total
        values = [v - mean for v in values]
        var = sum(jnp.sum(v * v, axis=1, keepdims=True) for v in values) / total
        scale = lax.rsqrt(var + 1e-05)
        for i, v in enumerate(values):
            cols = pl.ds(pl.multiple_of(place(i, parts) * width, width), width)
            normed_ref[at, cols] = (v * scale * gain_ref[:, cols]).astype(BF)
        out = jnp.dot(normed_ref[at, :], w_ref[...], preferred_element_type=F32)
        for pair in range(q_ref.shape[1] // TILE):
            a, b, c = [out[:, (3 * pair + i) * TILE : (3 * pair + i + 1) * TILE] for i in range(3)]
            q = pltpu.roll(jnp.where(lane < HD, a, b), HD, 1)
            q_ref[at, pair * TILE : (pair + 1) * TILE] = q.astype(BF)
            kv_ref[at, 2 * pair * TILE : (2 * pair + 1) * TILE] = jnp.where(lane < HD, b, a).astype(BF)
            kv_ref[at, (2 * pair + 1) * TILE : (2 * pair + 2) * TILE] = c.astype(BF)
        return carry

    lax.fori_loop(0, rows // block, step, 0)


def up_body(normed_ref, w_ref, exp_ref, out_ref):
    rows = normed_ref.shape[0]
    block = min(256, rows)
    cols = min(512, w_ref.shape[1])

    def step(k, carry):
        at = pl.ds(pl.multiple_of(k * block, block), block)
        for c in range(w_ref.shape[1] // cols):
            sl = slice(c * cols, (c + 1) * cols)
            up = jnp.dot(normed_ref[at, :], w_ref[:, sl], preferred_element_type=F32)
            up = up * power(exp_ref[:, sl])
            out_ref[at, sl] = (0.5 * up * (1.0 + lax.erf(up * 0.7071067811865476))).astype(BF)
        return carry

    lax.fori_loop(0, rows // block, step, 0)


def spot(which, b):
    n = WIN // BLOCK
    return jnp.where(parity() == which, b, n - 1 - b) * BLOCK


def slanted(which):
    i = lax.broadcasted_iota(jnp.int32, (BLOCK, BLOCK), 0)
    j = lax.broadcasted_iota(jnp.int32, (BLOCK, BLOCK), 1)
    return jnp.where(parity() == which, i - j, j - i)


def lane_ids():
    return lax.broadcasted_iota(jnp.int32, (BLOCK, TILE), 1)


def query_of(q_ref, pair, half):
    q = q_ref[:, pair * TILE : (pair + 1) * TILE] * BF(HD**-0.5)
    keep = (lane_ids() >= HD) if half == 0 else (lane_ids() < HD)
    return jnp.where(keep, q, jnp.zeros_like(q))


def scored(q, key):
    return lax.dot_general(q, key, (((1,), (1,)), ((), ())), preferred_element_type=F32)


def peak_of(scores):
    peak = scores[0]
    for s in scores[1:]:
        peak = jnp.maximum(peak, s)
    return jnp.max(peak, axis=1, keepdims=True)


def weighed(scores, peak, keys):
    probs = [jnp.exp(s - peak) for s in scores]
    total = probs[0]
    for p in probs[1:]:
        total = total + p
    mixed = jnp.dot(
        jnp.concatenate([p.astype(BF) for p in probs], axis=1),
        jnp.concatenate(keys, axis=0),
        preferred_element_type=F32,
    )
    return jnp.sum(total, axis=1, keepdims=True), mixed


def attend_body(which, b, q_ref, *refs):
    *refs, out_ref = refs
    bias = jnp.where(has_partner(which), 0.0, NEG).astype(F32)
    ahead = slanted(which)
    inner_mask = jnp.where(ahead <= 0, 0.0, NEG).astype(F32)
    outer_mask = jnp.where(ahead >= 0, bias, NEG).astype(F32)
    left = lane_ids() < HD
    for pair in range(q_ref.shape[1] // TILE):
        outs = []
        for half in range(2):
            cols = slice((2 * pair + half) * TILE, (2 * pair + half + 1) * TILE)
            q = query_of(q_ref, pair, half)
            keys = [ref[:, cols] for ref in refs]
            scores = [scored(q, key) for key in keys]
            scores[0] = scores[0] + inner_mask
            scores[4] = scores[4] + outer_mask
            if b == 1:
                scores[3] = scores[3] + bias
            total, mixed = weighed(scores, peak_of(scores), keys)
            outs.append(mixed / total)
        out_ref[:, pair * TILE : (pair + 1) * TILE] = jnp.where(left, outs[0], outs[1]).astype(BF)


def down_body(parts, n, *refs):
    atts, acts, (w_out_ref, w_down_ref, exp_ref), outs = (
        refs[:n],
        refs[n : 2 * n],
        refs[2 * n : 2 * n + 3],
        refs[2 * n + 3 :],
    )
    width = w_out_ref.shape[1] // parts
    for k in range(n):
        at = slice(k * BLOCK, (k + 1) * BLOCK)
        for i in range(parts):
            cols = pl.ds(pl.multiple_of(place(i, parts) * width, width), width)
            mlp = jnp.dot(acts[k][...], w_down_ref[:, cols], preferred_element_type=F32)
            att = jnp.dot(atts[k][...], w_out_ref[:, cols], preferred_element_type=F32)
            outs[i][at, :] = (att + mlp * power(exp_ref[:, cols])).astype(BF)


SWAP = [(0, 1), (1, 0)]
PIECES = ((0, 1), (0, 0), (1, 1), (1, 0))
UNITS = ((1, 0), (3,), (2,))


def gather(rows, split):
    if not split:
        return [lax.all_gather(rows, ("mp", "sub"), axis=1, tiled=True)]
    far = lax.ppermute(rows, "mp", SWAP)
    near = lax.ppermute(rows, "sub", SWAP)
    both = lax.ppermute(far, "sub", SWAP)
    return [rows, near, far, both]


def reduce_parts(parts, split):
    if not split:
        return [lax.psum_scatter(parts[0], ("mp", "sub"), scatter_dimension=1, tiled=True)]
    own, near, far, both = parts
    far_got = lax.ppermute(both, "sub", SWAP)
    near_got = lax.ppermute(near, "sub", SWAP)
    far_sum = (far.astype(F32) + far_got.astype(F32)).astype(BF)
    return [own, near_got, lax.ppermute(far_sum, "mp", SWAP)]


def settle_body(n, *refs):
    latents, adds, out = refs[:n], refs[n:-1], refs[-1]
    for k in range(n):
        at = slice(k * BLOCK, (k + 1) * BLOCK)
        total = adds[0][at, :].astype(F32)
        for term in adds[1:]:
            total = total + term[at, :].astype(F32)
        out[at, :] = (latents[k][...].astype(F32) + total).astype(BF)


def unit_starts(unit, count):
    return [start_of(*PIECES[g], count) for g in unit]


def unit_sources(unit, hidden_ref):
    return [hidden_ref.at[k * BLOCK : (k + 1) * BLOCK, :] for k in range(len(unit))]


def collect_body(side, units, count, part, weighted, earlier, src_ref, *refs):
    weight_ref, refs = (refs[0], refs[1:]) if weighted else (None, refs)
    hiddens, refs = refs[: len(units)], refs[len(units) :]
    n = {"sides": 2, "local": 1, "all": 3}[part]
    before, outs = refs[: n * earlier], refs[n * earlier :]
    before = list(before) or [None] * n
    sources, bases = [], []
    for unit, hidden_ref in zip(units, hiddens):
        sources += unit_sources(unit, hidden_ref)
        bases += unit_starts(unit, count)
    if part != "local":
        sides(side, src_ref, weight_ref, sources, bases, outs[:2], before[:2] if earlier else None)
    if part != "sides":
        locals_(2 * side, src_ref, weight_ref, sources, bases, outs[-1], before[-1])


def collect(side, units, count, part, edges, hiddens, before):
    features = hiddens[0].shape[1]
    out = jax.ShapeDtypeStruct((side * TILE, features), BF)
    local = jax.ShapeDtypeStruct(((edges[0].shape[0] - 2 * side) * TILE, features), BF)
    outs = {"sides": [out, out], "local": [local], "all": [out, out, local]}[part]
    return call(
        functools.partial(
            collect_body, side, units, count, part, len(edges) > 1, 1 if before else 0
        ),
        outs,
        (*edges, *hiddens, *before),
        2 * sum(h.size for h in hiddens) * sum(o.shape[0] for o in outs),
    )


def shards(
    grid_latent,
    grid_count,
    hidden_embed,
    enc_src_rows,
    enc_dst_rows,
    enc_weight,
    dec_src_rows,
    dec_dst_rows,
    dec_weight,
    norm_gain,
    w_qkv,
    w_out,
    w_up,
    up_exp,
    w_down,
    down_exp,
):
    split = lax.axis_size("mp") == 2 and lax.axis_size("sub") == 2
    parts = 4 if split else 1
    hid_rows, features = hidden_embed.shape
    full = w_qkv.shape[0]
    heads = w_qkv.shape[1] // (3 * HD)
    units = w_up.shape[1]
    rows = WIN
    count = hid_rows // rows
    assert count == 2
    src, dst, wts = enc_src_rows[0], enc_dst_rows[0], enc_weight[0]
    out = jax.ShapeDtypeStruct((ESIDE * TILE, features), BF)
    args = (src, wts, grid_latent)
    leaving = call(
        functools.partial(fetch_side_body, ESIDE),
        (out, out),
        args,
        4 * ESIDE * TILE * grid_latent.size,
        scratch=[
            *(pltpu.VMEM(a.shape, a.dtype) for a in args),
            pltpu.SemaphoreType.DMA((len(args),)),
        ],
        space=pltpu.HBM,
        limit=60 * 1024 * 1024,
    )
    arrived = swapped(*leaving)
    moved = gathered(src, wts, grid_latent, ESIDE)
    total = spread(dst, moved, hid_rows, ESIDE)
    latents, gathers = [], []
    for c, b in PIECES:
        (latent,) = call(
            functools.partial(latent_body, ESIDE, c, b, count),
            (jax.ShapeDtypeStruct((BLOCK, features), BF),),
            (dst, *arrived, total, hidden_embed),
            4 * ESIDE * TILE * BLOCK * features,
        )
        latents.append(latent)
        gathers.append(gather(latent, split))
    links = partners(lax.axis_size("seq"), lax.axis_size("ens"))
    queries, kvs, outer, activated = [], [], [], []
    for g, (c, b) in enumerate(PIECES):
        normed, q, part = call(
            functools.partial(qkv_body, parts),
            (
                jax.ShapeDtypeStruct((BLOCK, full), BF),
                jax.ShapeDtypeStruct((BLOCK, heads * HD), BF),
                jax.ShapeDtypeStruct((BLOCK, 2 * heads * HD), BF),
            ),
            (*gathers[g], norm_gain[None, :], w_qkv),
            2 * BLOCK * w_qkv.size,
        )
        queries.append(q)
        kvs.append(part)
        outer.append(lax.ppermute(part, ("ens", "seq"), links[c]))
        (act,) = call(
            up_body,
            (jax.ShapeDtypeStruct((BLOCK, units), BF),),
            (normed, w_up, up_exp[None, :]),
            2 * BLOCK * w_up.size,
        )
        activated.append(act)
    attended = []
    for g, (c, b) in enumerate(PIECES):
        o, h = 2 * (1 - c), 2 * c
        keys = (kvs[o], kvs[o + 1], kvs[h + 1], kvs[h], outer[h], outer[h + 1])[b : b + 5]
        (att,) = call(
            functools.partial(attend_body, c, b),
            (jax.ShapeDtypeStruct((BLOCK, heads * HD), BF),),
            (queries[g], *keys),
            4 * BLOCK * 5 * BLOCK * heads * HD,
            spare=12,
        )
        attended.append(att)
    src, dst, wts = dec_src_rows[0], dec_dst_rows[0], dec_weight[0]
    hiddens = []
    for unit in UNITS:
        size = len(unit) * BLOCK
        outs = call(
            functools.partial(down_body, parts, len(unit)),
            [jax.ShapeDtypeStruct((size, full // parts), BF)] * parts,
            (
                *(attended[g] for g in unit),
                *(activated[g] for g in unit),
                w_out,
                w_down,
                down_exp[None, :],
            ),
            2 * size * (w_out.size + w_down.size),
        )
        sums = reduce_parts(outs, split)
        (hidden,) = call(
            functools.partial(settle_body, len(unit)),
            (jax.ShapeDtypeStruct((size, features), BF),),
            (*(latents[g] for g in unit), *sums),
            4 * size * features,
        )
        hiddens.append(hidden)
    before = collect(DSIDE, UNITS[:1], count, "all", (src,), hiddens[:1], ())
    args = (src, wts)
    leaving = collect(DSIDE, UNITS[1:], count, "sides", args, hiddens[1:], before[:2])
    arrived = swapped(*leaving)
    (moved,) = collect(DSIDE, UNITS[1:], count, "local", args, hiddens[1:], before[2:])
    total = spread(dst, moved, grid_latent.shape[0], DSIDE)
    return settled(DSIDE, count, grid_count[None, :], dst, *arrived, total, grid_latent, hiddens)


def solution(mesh):
    placed = (
        P(("ens", "seq"), ("mp", "sub")),
        P(("ens", "seq")),
        P(("ens", "seq"), ("mp", "sub")),
        P(("ens", "seq"), None, None),
        P(("ens", "seq"), None, None),
        P(("ens", "seq"), None, None),
        P(("ens", "seq"), None, None),
        P(("ens", "seq"), None, None),
        P(("ens", "seq"), None, None),
        P(),
        P(None, ("mp", "sub")),
        P(("mp", "sub"), None),
        P(None, ("mp", "sub")),
        P(("mp", "sub")),
        P(("mp", "sub"), None),
        P(),
    )
    return jax.shard_map(
        shards,
        mesh=mesh,
        in_specs=placed,
        out_specs=(P(("ens", "seq"), ("mp", "sub")), P(("ens", "seq"), ("mp", "sub"))),
        check_vma=False,
    )
```

```python
import functools

import jax
import jax.numpy as jnp
from jax import lax
from jax.experimental import pallas as pl
from jax.experimental.pallas import tpu as pltpu
from jax.sharding import PartitionSpec as P

HD = 64
WIN = 512
TILE = 128
ESIDE = 4
DSIDE = 4
STEP = 4
BLOCK = 256
NEG = -1e30
LOG2E = 1.4426950408889634
BF = jnp.bfloat16
F32 = jnp.float32


def call(body, outs, args, flops, scratch=(), spare=8, space=pltpu.VMEM, out_space=pltpu.VMEM, limit=None):
    moved = sum(a.size * a.dtype.itemsize for a in args)
    moved += sum(o.size * o.dtype.itemsize for o in outs)
    return pl.pallas_call(
        body,
        out_shape=tuple(outs),
        in_specs=[pl.BlockSpec(memory_space=space)] * len(args),
        out_specs=tuple(pl.BlockSpec(memory_space=out_space) for _ in outs),
        scratch_shapes=list(scratch),
        cost_estimate=pl.CostEstimate(flops=flops, bytes_accessed=moved, transcendentals=0),
        compiler_params=pltpu.CompilerParams(vmem_limit_bytes=limit or moved + spare * 1024 * 1024),
    )(*args)


def column(row):
    return jnp.transpose(jnp.broadcast_to(row, (TILE, TILE)))


def columns(rows_ref, first):
    tiles = [column(rows_ref[pl.ds(first + i, 1), :]) for i in range(STEP)]
    return jnp.concatenate(tiles, axis=0).astype(jnp.int16)


def picks(cols, base, source_rows):
    cols = cols - jnp.asarray(base, jnp.int32).astype(jnp.int16)
    lane = lax.broadcasted_iota(jnp.int32, cols.shape, 1).astype(jnp.int16)
    tiles = []
    for j in range(source_rows // TILE):
        hit = cols == lane + jnp.int16(j * TILE)
        tiles.append(jnp.where(hit, jnp.ones_like(cols, BF), jnp.zeros_like(cols, BF)))
    return jnp.concatenate(tiles, axis=1)


def picked(cols, sources, bases):
    total = None
    for source_ref, base in zip(sources, bases):
        part = jnp.dot(
            picks(cols, base, source_ref.shape[0]), source_ref[...], preferred_element_type=F32
        )
        total = part if total is None else total + part
    return total


def scaled(rows, weight_ref, first):
    scale = jnp.concatenate([column(weight_ref[pl.ds(first + i, 1), :]) for i in range(STEP)], axis=0)
    return (rows * jnp.concatenate([scale] * (rows.shape[1] // TILE), axis=1)).astype(BF)


def parity():
    return lax.rem(lax.axis_index("seq"), 2)


def outward(which, side):
    return jnp.where(parity() == which, side, 0)


def block_of(step, count):
    return step if count == 1 else jnp.where(parity() == 0, count - 1 - step, step)


def partners(count, groups):
    both = []
    for which in range(2):
        pairs = []
        for e in range(groups):
            for i in range(count):
                j = ((i - which) ^ 1) + which
                if 0 <= j < count:
                    pairs.append((e * count + i, e * count + j))
                elif e ^ 1 < groups:
                    pairs.append((e * count + i, (e ^ 1) * count + i))
        both.append(pairs)
    return both


def has_partner(which):
    seq = lax.axis_index("seq")
    return jnp.where(parity() == which, seq < lax.axis_size("seq") - 1, seq > 0)


def sides(side, src_ref, weight_ref, sources, bases, outs, before=None):
    edges = STEP * TILE
    for which, out in enumerate(outs):
        for k in range(out.shape[0] // edges):
            at = slice(k * edges, (k + 1) * edges)
            first = outward(which, side) + k * STEP
            rows = picked(columns(src_ref, first), sources, bases)
            if before is not None:
                rows = rows + before[which][at, :].astype(F32)
            out[at, :] = rows.astype(BF) if weight_ref is None else scaled(rows, weight_ref, first)


def fetch_side_body(side, *refs):
    (src_ref, weight_ref, source_ref), outs, refs = refs[:3], refs[3:5], refs[5:]
    src, weight, source, *made, sems = refs
    half = source_ref.shape[0] // 2
    loads = [
        pltpu.make_async_copy(src_ref, src, sems.at[0]),
        pltpu.make_async_copy(weight_ref, weight, sems.at[1]),
    ]
    for i in range(2):
        at = slice(i * half, (i + 1) * half)
        loads.append(pltpu.make_async_copy(source_ref.at[at, :], source.at[at, :], sems.at[2 + i]))
    for load in loads:
        load.start()
    loads[0].wait()
    edges = STEP * TILE
    firsts = [
        (which, k, outward(which, side) + k * STEP)
        for which, value_ref in enumerate(made)
        for k in range(value_ref.shape[0] // edges)
    ]
    cols = [columns(src, first) for _, _, first in firsts]
    loads[1].wait()
    totals = [None] * len(firsts)
    for i in range(2):
        loads[2 + i].wait()
        at = slice(i * half, (i + 1) * half)
        for n, col in enumerate(cols):
            part = picked(col, (source.at[at, :],), (i * half,))
            totals[n] = part if totals[n] is None else totals[n] + part
    stores = []
    for (which, k, first), total in zip(firsts, totals):
        made[which][k * edges : (k + 1) * edges, :] = scaled(total, weight, first)
        if (k + 1) * edges == made[which].shape[0]:
            stores.append(pltpu.make_async_copy(made[which], outs[which], sems.at[4 + which]))
            stores[-1].start()
    for store in stores:
        store.wait()


def locals_(start, src_ref, weight_ref, sources, bases, out_ref, before_ref, keep_ref, kept_ref):
    edges = STEP * TILE
    pair = 5 if out_ref.shape[0] % (5 * edges) == 0 else 2

    def step(k, carry):
        for i in range(pair):
            n = k * pair + i
            at = pl.ds(pl.multiple_of(n * edges, edges), edges)
            first = start + n * STEP
            cols = columns(src_ref, first) if kept_ref is None else kept_ref[at, :]
            if keep_ref is not None:
                keep_ref[at, :] = cols
            rows = picked(cols, sources, bases)
            if before_ref is not None:
                rows = rows + before_ref[at, :].astype(F32)
            out_ref[at, :] = rows.astype(BF) if weight_ref is None else scaled(rows, weight_ref, first)
        return carry

    lax.fori_loop(0, out_ref.shape[0] // (pair * edges), step, 0)


def gather_body(start, src_ref, weight_ref, source_ref, out_ref):
    locals_(start, src_ref, weight_ref, (source_ref,), (0,), out_ref, None, None, None)


def lands(rows_ref, tiles, base, target_rows, there=None):
    spot = lax.broadcasted_iota(jnp.int32, (target_rows, TILE), 0).astype(jnp.int16)
    out = []
    for tile in tiles:
        row = rows_ref[pl.ds(tile, 1), :] - base
        row = row if there is None else jnp.where(there, row, -1)
        row = jnp.broadcast_to(row, (target_rows, TILE)).astype(jnp.int16)
        out.append(jnp.where(row == spot, jnp.ones_like(spot, BF), jnp.zeros_like(spot, BF)))
    return jnp.concatenate(out, axis=1)


def landed(side, dst_ref, first_ref, second_ref, base, target_rows):
    total = None
    for which, got_ref in enumerate((first_ref, second_ref)):
        first = outward(which, side)
        got = jnp.dot(
            lands(dst_ref, [first + i for i in range(side)], base, target_rows, has_partner(which)),
            got_ref[...],
            preferred_element_type=F32,
        )
        total = got if total is None else total + got
    return total


def spread_body(side, dst_ref, local_ref, out_ref):
    block = 512

    def step(k, carry):
        for i in range(2):
            at = pl.multiple_of((2 * k + i) * block, block)
            tiles = [2 * side + t for t in range(local_ref.shape[0] // TILE)]
            out_ref[pl.ds(at, block), :] = jnp.dot(
                lands(dst_ref, tiles, at, block), local_ref[...], preferred_element_type=F32
            )
        return carry

    lax.fori_loop(0, out_ref.shape[0] // (2 * block), step, 0)


def start_of(c, b, count):
    return block_of(c, count) * WIN + spot(c, b)


def latent_body(side, c, b, count, dst_ref, first_ref, second_ref, total_ref, embed_ref, out_ref):
    at = pl.multiple_of(start_of(c, b, count), BLOCK)
    got = landed(side, dst_ref, first_ref, second_ref, at, BLOCK)
    got = got + total_ref[pl.ds(at, BLOCK), :]
    out_ref[...] = (embed_ref[pl.ds(at, BLOCK), :].astype(F32) + got).astype(BF)


def grid_body(side, count, count_ref, dst_ref, first_ref, second_ref, total_ref, grid_ref, *refs):
    *hiddens, hidden_ref, out_ref = refs
    rows = out_ref.shape[0]
    step = pl.program_id(0)
    for h in range(rows // BLOCK):
        at = pl.multiple_of(step * rows + h * BLOCK, BLOCK)
        here = slice(h * BLOCK, (h + 1) * BLOCK)
        from_ = pl.ds(at, BLOCK)
        got = landed(side, dst_ref, first_ref, second_ref, at, BLOCK) + total_ref[from_, :]
        row = at + lax.broadcasted_iota(jnp.int32, got.shape, 0)
        value = grid_ref[from_, :].astype(F32) + got
        out_ref[here, :] = jnp.where(row < count_ref[0, 0], value, 0.0).astype(BF)
    for c, chunk_ref in enumerate(hiddens):
        n = WIN // BLOCK

        @pl.when(step // n == block_of(c, count))
        def _():
            hidden_ref[...] = chunk_ref[pl.ds(pl.multiple_of(step % n * BLOCK, BLOCK), BLOCK), :]


def swapped(first, second):
    one, two = partners(lax.axis_size("seq"), lax.axis_size("ens"))
    axes = ("ens", "seq")
    return lax.ppermute(first, axes, one), lax.ppermute(second, axes, two)


def gathered(edge_src, edge_weight, source, side):
    edges = edge_src.shape[0] * TILE - 2 * side * TILE
    (local,) = call(
        functools.partial(gather_body, 2 * side),
        (jax.ShapeDtypeStruct((edges, source.shape[1]), BF),),
        (edge_src, edge_weight, source),
        2 * edges * source.size,
    )
    return local


def spread(edge_dst, local, target_rows, side):
    (total,) = call(
        functools.partial(spread_body, side),
        (jax.ShapeDtypeStruct((target_rows, local.shape[1]), F32),),
        (edge_dst, local),
        2 * local.size * target_rows,
    )
    return total


def settled(side, count, grid_count, edge_dst, first, second, total, grid_latent, hiddens):
    rows, features = grid_latent.shape
    steps = sum(h.shape[0] for h in hiddens) // BLOCK
    block = rows // steps
    args = (grid_count, edge_dst, first, second, total, grid_latent, *hiddens)
    return pl.pallas_call(
        functools.partial(grid_body, side, count),
        grid=(steps,),
        out_shape=(
            jax.ShapeDtypeStruct((steps * BLOCK, features), BF),
            jax.ShapeDtypeStruct((rows, features), BF),
        ),
        in_specs=[pl.BlockSpec(memory_space=pltpu.VMEM)] * len(args),
        out_specs=(
            pl.BlockSpec((BLOCK, features), lambda i: (i, 0)),
            pl.BlockSpec((block, features), lambda i: (i, 0)),
        ),
        cost_estimate=pl.CostEstimate(
            flops=4 * side * TILE * grid_latent.size,
            bytes_accessed=8 * grid_latent.size,
            transcendentals=0,
        ),
        compiler_params=pltpu.CompilerParams(vmem_limit_bytes=16 * 1024 * 1024),
        name="grid",
    )(*args)


def power(exponent):
    return jnp.where(exponent > 0, 2.0, jnp.where(exponent < 0, 0.5, 1.0)).astype(F32)


def place(step, parts):
    if parts == 1:
        return 0
    mp = lax.axis_index("mp")
    sub = lax.axis_index("sub")
    mp = mp if step < 2 else 1 - mp
    sub = sub if step % 2 == 0 else 1 - sub
    return 2 * mp + sub


def qkv_body(parts, *refs):
    pieces, (gain_ref, w_ref, *refs) = refs[:parts], refs[parts:]
    normed_ref, q_ref, kv_ref = refs
    rows, width = pieces[0].shape
    total = width * parts
    block = min(256, rows)
    lane = lax.broadcasted_iota(jnp.int32, (block, TILE), 1)

    def step(k, carry):
        at = pl.ds(pl.multiple_of(k * block, block), block)
        values = [p[at, :].astype(F32) for p in pieces]
        mean = sum(jnp.sum(v, axis=1, keepdims=True) for v in values) / total
        values = [v - mean for v in values]
        var = sum(jnp.sum(v * v, axis=1, keepdims=True) for v in values) / total
        scale = lax.rsqrt(var + 1e-05)
        for i, v in enumerate(values):
            cols = pl.ds(pl.multiple_of(place(i, parts) * width, width), width)
            normed_ref[at, cols] = (v * scale * gain_ref[:, cols]).astype(BF)
        out = jnp.dot(normed_ref[at, :], w_ref[...], preferred_element_type=F32)
        for pair in range(q_ref.shape[1] // TILE):
            a, b, c = [out[:, (3 * pair + i) * TILE : (3 * pair + i + 1) * TILE] for i in range(3)]
            q = pltpu.roll(jnp.where(lane < HD, a, b), HD, 1) * (HD**-0.5 * LOG2E)
            q_ref[at, pair * TILE : (pair + 1) * TILE] = q.astype(BF)
            kv_ref[at, 2 * pair * TILE : (2 * pair + 1) * TILE] = jnp.where(lane < HD, b, a).astype(BF)
            kv_ref[at, (2 * pair + 1) * TILE : (2 * pair + 2) * TILE] = c.astype(BF)
        return carry

    lax.fori_loop(0, rows // block, step, 0)


def up_body(normed_ref, w_ref, exp_ref, out_ref):
    rows = normed_ref.shape[0]
    block = min(256, rows)
    cols = min(512, w_ref.shape[1])

    def step(k, carry):
        at = pl.ds(pl.multiple_of(k * block, block), block)
        for c in range(w_ref.shape[1] // cols):
            sl = slice(c * cols, (c + 1) * cols)
            up = jnp.dot(normed_ref[at, :], w_ref[:, sl], preferred_element_type=F32)
            up = up * power(exp_ref[:, sl])
            out_ref[at, sl] = (0.5 * up * (1.0 + lax.erf(up * 0.7071067811865476))).astype(BF)
        return carry

    lax.fori_loop(0, rows // block, step, 0)


def spot(which, b):
    n = WIN // BLOCK
    return jnp.where(parity() == which, b, n - 1 - b) * BLOCK


def slanted(which):
    i = lax.broadcasted_iota(jnp.int32, (BLOCK, BLOCK), 0)
    j = lax.broadcasted_iota(jnp.int32, (BLOCK, BLOCK), 1)
    return jnp.where(parity() == which, i - j, j - i)


def lane_ids():
    return lax.broadcasted_iota(jnp.int32, (BLOCK, TILE), 1)


def query_of(q_ref, pair, half):
    q = q_ref[:, pair * TILE : (pair + 1) * TILE]
    keep = (lane_ids() >= HD) if half == 0 else (lane_ids() < HD)
    return jnp.where(keep, q, jnp.zeros_like(q))


def scored(q, key):
    return lax.dot_general(q, key, (((1,), (1,)), ((), ())), preferred_element_type=F32)


def peak_of(scores):
    peak = scores[0]
    for s in scores[1:]:
        peak = jnp.maximum(peak, s)
    return jnp.max(peak, axis=1, keepdims=True)


def attend_body(which, b, q_ref, *refs):
    *refs, out_ref = refs
    bias = jnp.where(has_partner(which), 0.0, NEG).astype(F32)
    ahead = slanted(which)
    inner_mask = jnp.where(ahead <= 0, 0.0, NEG).astype(F32)
    outer_mask = jnp.where(ahead >= 0, bias, NEG).astype(F32)
    left = lane_ids() < HD
    jobs = [(pair, half) for pair in range(q_ref.shape[1] // TILE) for half in range(2)]

    def scores_of(pair, half):
        cols = slice((2 * pair + half) * TILE, (2 * pair + half + 1) * TILE)
        q = query_of(q_ref, pair, half)
        keys = [ref[:, cols] for ref in refs]
        scores = [scored(q, key) for key in keys]
        scores[0] = scores[0] + inner_mask
        scores[4] = scores[4] + outer_mask
        if b == 1:
            scores[3] = scores[3] + bias
        return keys, scores

    outs = []
    ready = scores_of(*jobs[0])
    for n, (pair, half) in enumerate(jobs):
        keys, scores = ready
        if n + 1 < len(jobs):
            ready = scores_of(*jobs[n + 1])
        peak = peak_of(scores)
        probs = jnp.concatenate([jnp.exp2(s - peak).astype(BF) for s in scores], axis=1)
        keep = left if half == 0 else jnp.logical_not(left)
        values = [jnp.where(keep, key, jnp.ones_like(key)) for key in keys]
        outs.append(jnp.dot(probs, jnp.concatenate(values, axis=0), preferred_element_type=F32))
        if half:
            sums = pltpu.roll(jnp.where(left, outs[1], outs[0]), HD, 1)
            mixed = jnp.where(left, outs[0], outs[1])
            out_ref[:, pair * TILE : (pair + 1) * TILE] = (mixed / sums).astype(BF)
            outs = []


def down_body(parts, n, *refs):
    atts, acts, (w_out_ref, w_down_ref, exp_ref), outs = (
        refs[:n],
        refs[n : 2 * n],
        refs[2 * n : 2 * n + 3],
        refs[2 * n + 3 :],
    )
    width = w_out_ref.shape[1] // parts
    for k in range(n):
        at = slice(k * BLOCK, (k + 1) * BLOCK)
        for i in range(parts):
            cols = pl.ds(pl.multiple_of(place(i, parts) * width, width), width)
            mlp = jnp.dot(acts[k][...], w_down_ref[:, cols], preferred_element_type=F32)
            att = jnp.dot(atts[k][...], w_out_ref[:, cols], preferred_element_type=F32)
            outs[i][at, :] = (att + mlp * power(exp_ref[:, cols])).astype(BF)


SWAP = [(0, 1), (1, 0)]
PIECES = ((0, 1), (0, 0), (1, 1), (1, 0))
UNITS = ((1, 0), (3,), (2,))


def gather(rows, split):
    if not split:
        return [lax.all_gather(rows, ("mp", "sub"), axis=1, tiled=True)]
    far = lax.ppermute(rows, "mp", SWAP)
    near = lax.ppermute(rows, "sub", SWAP)
    both = lax.ppermute(far, "sub", SWAP)
    return [rows, near, far, both]


def reduce_parts(parts, split):
    if not split:
        return [lax.psum_scatter(parts[0], ("mp", "sub"), scatter_dimension=1, tiled=True)]
    own, near, far, both = parts
    far_got = lax.ppermute(both, "sub", SWAP)
    near_got = lax.ppermute(near, "sub", SWAP)
    far_sum = (far.astype(F32) + far_got.astype(F32)).astype(BF)
    return [own, near_got, lax.ppermute(far_sum, "mp", SWAP)]


def settle_body(unit, *refs):
    n = len(unit)
    latents, (*adds, out) = refs[:n], refs[n:]
    if out.shape[0] > n * BLOCK:
        earlier_ref, *adds = adds
        other = spot(PIECES[unit[0]][0], 1 - PIECES[unit[0]][1])
        out[pl.ds(pl.multiple_of(other, BLOCK), BLOCK), :] = earlier_ref[...]
    for k, g in enumerate(unit):
        at = slice(k * BLOCK, (k + 1) * BLOCK)
        total = adds[0][at, :].astype(F32)
        for term in adds[1:]:
            total = total + term[at, :].astype(F32)
        start = 0 if out.shape[0] == BLOCK else spot(*PIECES[g])
        spots = pl.ds(pl.multiple_of(start, BLOCK), BLOCK) if out.shape[0] > BLOCK else slice(None)
        out[spots, :] = (latents[k][...].astype(F32) + total).astype(BF)


def leave_body(side, c, count, src_ref, *refs):
    last = c == count - 1
    weight_ref, refs = (refs[0], refs[1:]) if last else (None, refs)
    hidden_ref, before, outs = refs[:1], refs[1:-2], refs[-2:]
    sides(side, src_ref, weight_ref, hidden_ref, (block_of(c, count) * WIN,), outs, before or None)


def stay_body(side, c, count, src_ref, *refs):
    base = (block_of(c, count) * WIN,)
    if c == count - 1:
        weight_ref, hidden_ref, before_ref, kept_ref, out_ref = refs
        locals_(
            2 * side, src_ref, weight_ref, (hidden_ref,), base, out_ref, before_ref, None, kept_ref
        )
    else:
        hidden_ref, out_ref, keep_ref = refs
        locals_(2 * side, src_ref, None, (hidden_ref,), base, out_ref, None, keep_ref, None)


def leaving(side, c, count, args, hidden, before):
    out = jax.ShapeDtypeStruct((side * TILE, hidden.shape[1]), BF)
    return call(
        functools.partial(leave_body, side, c, count),
        (out, out),
        (*args, hidden, *before),
        4 * side * TILE * hidden.size,
    )


def staying(side, c, count, args, hidden, before):
    edges = (args[0].shape[0] - 2 * side) * TILE
    outs = [jax.ShapeDtypeStruct((edges, hidden.shape[1]), BF)]
    if not before:
        outs.append(jax.ShapeDtypeStruct((edges, TILE), jnp.int16))
    return call(
        functools.partial(stay_body, side, c, count),
        outs,
        (*args, hidden, *before),
        2 * edges * hidden.size,
    )


def shards(
    grid_latent,
    grid_count,
    hidden_embed,
    enc_src_rows,
    enc_dst_rows,
    enc_weight,
    dec_src_rows,
    dec_dst_rows,
    dec_weight,
    norm_gain,
    w_qkv,
    w_out,
    w_up,
    up_exp,
    w_down,
    down_exp,
):
    split = lax.axis_size("mp") == 2 and lax.axis_size("sub") == 2
    parts = 4 if split else 1
    hid_rows, features = hidden_embed.shape
    full = w_qkv.shape[0]
    heads = w_qkv.shape[1] // (3 * HD)
    units = w_up.shape[1]
    rows = WIN
    count = hid_rows // rows
    assert count == 2
    src, dst, wts = enc_src_rows[0], enc_dst_rows[0], enc_weight[0]
    out = jax.ShapeDtypeStruct((ESIDE * TILE, features), BF)
    args = (src, wts, grid_latent)
    out = call(
        functools.partial(fetch_side_body, ESIDE),
        (out, out),
        args,
        4 * ESIDE * TILE * grid_latent.size,
        scratch=[
            *(pltpu.VMEM(a.shape, a.dtype) for a in (*args, out, out)),
            pltpu.SemaphoreType.DMA((6,)),
        ],
        space=pltpu.HBM,
        out_space=pltpu.HBM,
        limit=60 * 1024 * 1024,
    )
    arrived = swapped(*out)
    moved = gathered(src, wts, grid_latent, ESIDE)
    total = spread(dst, moved, hid_rows, ESIDE)
    latents, gathers = [], []
    for c, b in PIECES:
        (latent,) = call(
            functools.partial(latent_body, ESIDE, c, b, count),
            (jax.ShapeDtypeStruct((BLOCK, features), BF),),
            (dst, *arrived, total, hidden_embed),
            4 * ESIDE * TILE * BLOCK * features,
        )
        latents.append(latent)
        gathers.append(gather(latent, split))
    links = partners(lax.axis_size("seq"), lax.axis_size("ens"))
    queries, kvs, outer, activated = [], [], [], []
    for g, (c, b) in enumerate(PIECES):
        normed, q, part = call(
            functools.partial(qkv_body, parts),
            (
                jax.ShapeDtypeStruct((BLOCK, full), BF),
                jax.ShapeDtypeStruct((BLOCK, heads * HD), BF),
                jax.ShapeDtypeStruct((BLOCK, 2 * heads * HD), BF),
            ),
            (*gathers[g], norm_gain[None, :], w_qkv),
            2 * BLOCK * w_qkv.size,
        )
        queries.append(q)
        kvs.append(part)
        outer.append(lax.ppermute(part, ("ens", "seq"), links[c]))
        (act,) = call(
            up_body,
            (jax.ShapeDtypeStruct((BLOCK, units), BF),),
            (normed, w_up, up_exp[None, :]),
            2 * BLOCK * w_up.size,
        )
        activated.append(act)
    attended = []
    for g, (c, b) in enumerate(PIECES):
        o, h = 2 * (1 - c), 2 * c
        keys = (kvs[o], kvs[o + 1], kvs[h + 1], kvs[h], outer[h], outer[h + 1])[b : b + 5]
        (att,) = call(
            functools.partial(attend_body, c, b),
            (jax.ShapeDtypeStruct((BLOCK, heads * HD), BF),),
            (queries[g], *keys),
            4 * BLOCK * 5 * BLOCK * heads * HD,
            spare=12,
        )
        attended.append(att)
    src, dst, wts = dec_src_rows[0], dec_dst_rows[0], dec_weight[0]
    hiddens = []
    for u, unit in enumerate(UNITS):
        size = len(unit) * BLOCK
        outs = call(
            functools.partial(down_body, parts, len(unit)),
            [jax.ShapeDtypeStruct((size, full // parts), BF)] * parts,
            (
                *(attended[g] for g in unit),
                *(activated[g] for g in unit),
                w_out,
                w_down,
                down_exp[None, :],
            ),
            2 * size * (w_out.size + w_down.size),
        )
        sums = reduce_parts(outs, split)
        earlier = hiddens[-1:] if u == len(UNITS) - 1 else []
        (hidden,) = call(
            functools.partial(settle_body, unit),
            (jax.ShapeDtypeStruct((size + len(earlier) * BLOCK, features), BF),),
            (*(latents[g] for g in unit), *earlier, *sums),
            4 * size * features,
        )
        hiddens.append(hidden)
    hiddens = [hiddens[0], hiddens[-1]]
    before = leaving(DSIDE, 0, count, (src,), hiddens[0], ())
    kept = staying(DSIDE, 0, count, (src,), hiddens[0], ())
    args = (src, wts)
    arrived = swapped(*leaving(DSIDE, 1, count, args, hiddens[1], before))
    (moved,) = staying(DSIDE, 1, count, args, hiddens[1], kept)
    total = spread(dst, moved, grid_latent.shape[0], DSIDE)
    return settled(DSIDE, count, grid_count[None, :], dst, *arrived, total, grid_latent, hiddens)


def solution(mesh):
    placed = (
        P(("ens", "seq"), ("mp", "sub")),
        P(("ens", "seq")),
        P(("ens", "seq"), ("mp", "sub")),
        P(("ens", "seq"), None, None),
        P(("ens", "seq"), None, None),
        P(("ens", "seq"), None, None),
        P(("ens", "seq"), None, None),
        P(("ens", "seq"), None, None),
        P(("ens", "seq"), None, None),
        P(),
        P(None, ("mp", "sub")),
        P(("mp", "sub"), None),
        P(None, ("mp", "sub")),
        P(("mp", "sub")),
        P(("mp", "sub"), None),
        P(),
    )
    return jax.shard_map(
        shards,
        mesh=mesh,
        in_specs=placed,
        out_specs=(P(("ens", "seq"), ("mp", "sub")), P(("ens", "seq"), ("mp", "sub"))),
        check_vma=False,
    )
```

```python
import functools

import jax
import jax.numpy as jnp
from jax import lax
from jax.experimental import pallas as pl
from jax.experimental.pallas import tpu as pltpu
from jax.sharding import PartitionSpec as P

HD = 64
WIN = 512
TILE = 128
ESIDE = 4
DSIDE = 4
STEP = 4
BLOCK = 256
NEG = -1e30
LOG2E = 1.4426950408889634
BF = jnp.bfloat16
F32 = jnp.float32


def call(body, outs, args, flops, scratch=(), spare=8, space=pltpu.VMEM, out_space=pltpu.VMEM, last_space=None, limit=None):
    moved = sum(a.size * a.dtype.itemsize for a in args)
    moved += sum(o.size * o.dtype.itemsize for o in outs)
    return pl.pallas_call(
        body,
        out_shape=tuple(outs),
        in_specs=[pl.BlockSpec(memory_space=space)] * len(args),
        out_specs=tuple(
            pl.BlockSpec(memory_space=(out_space if i == 0 else last_space or out_space))
            for i in range(len(outs))
        ),
        scratch_shapes=list(scratch),
        cost_estimate=pl.CostEstimate(flops=flops, bytes_accessed=moved, transcendentals=0),
        compiler_params=pltpu.CompilerParams(vmem_limit_bytes=limit or moved + spare * 1024 * 1024),
    )(*args)


def column(row):
    return jnp.transpose(jnp.broadcast_to(row, (TILE, TILE)))


def columns(rows_ref, first):
    tiles = [column(rows_ref[pl.ds(first + i, 1), :]) for i in range(STEP)]
    return jnp.concatenate(tiles, axis=0).astype(jnp.int16)


def picks(cols, base, source_rows):
    cols = cols - jnp.asarray(base, jnp.int32).astype(jnp.int16)
    lane = lax.broadcasted_iota(jnp.int32, cols.shape, 1).astype(jnp.int16)
    tiles = []
    for j in range(source_rows // TILE):
        hit = cols == lane + jnp.int16(j * TILE)
        tiles.append(jnp.where(hit, jnp.ones_like(cols, BF), jnp.zeros_like(cols, BF)))
    return jnp.concatenate(tiles, axis=1)


def picked(cols, sources, bases):
    total = None
    for source_ref, base in zip(sources, bases):
        part = jnp.dot(
            picks(cols, base, source_ref.shape[0]), source_ref[...], preferred_element_type=F32
        )
        total = part if total is None else total + part
    return total


def scaled(rows, weight_ref, first):
    scale = jnp.concatenate([column(weight_ref[pl.ds(first + i, 1), :]) for i in range(STEP)], axis=0)
    return (rows * jnp.concatenate([scale] * (rows.shape[1] // TILE), axis=1)).astype(BF)


def parity():
    return lax.rem(lax.axis_index("seq"), 2)


def outward(which, side):
    return jnp.where(parity() == which, side, 0)


def block_of(step, count):
    return step if count == 1 else jnp.where(parity() == 0, count - 1 - step, step)


def partners(count, groups):
    both = []
    for which in range(2):
        pairs = []
        for e in range(groups):
            for i in range(count):
                j = ((i - which) ^ 1) + which
                if 0 <= j < count:
                    pairs.append((e * count + i, e * count + j))
                elif e ^ 1 < groups:
                    pairs.append((e * count + i, (e ^ 1) * count + i))
        both.append(pairs)
    return both


def has_partner(which):
    seq = lax.axis_index("seq")
    return jnp.where(parity() == which, seq < lax.axis_size("seq") - 1, seq > 0)


def sides(side, src_ref, weight_ref, sources, bases, outs, before=None):
    edges = STEP * TILE
    for which, out in enumerate(outs):
        for k in range(out.shape[0] // edges):
            at = slice(k * edges, (k + 1) * edges)
            first = outward(which, side) + k * STEP
            rows = picked(columns(src_ref, first), sources, bases)
            if before is not None:
                rows = rows + before[which][at, :].astype(F32)
            out[at, :] = rows.astype(BF) if weight_ref is None else scaled(rows, weight_ref, first)


def fetch_side_body(side, *refs):
    (src_ref, weight_ref, source_ref), outs, refs = refs[:3], refs[3:5], refs[5:]
    src, weight, source, *made, sems = refs
    half = source_ref.shape[0] // 2
    loads = [
        pltpu.make_async_copy(src_ref, src, sems.at[0]),
        pltpu.make_async_copy(weight_ref, weight, sems.at[1]),
    ]
    for i in range(2):
        at = slice(i * half, (i + 1) * half)
        loads.append(pltpu.make_async_copy(source_ref.at[at, :], source.at[at, :], sems.at[2 + i]))
    for load in loads:
        load.start()
    loads[0].wait()
    edges = STEP * TILE
    firsts = [
        (which, k, outward(which, side) + k * STEP)
        for which, value_ref in enumerate(made)
        for k in range(value_ref.shape[0] // edges)
    ]
    cols = [columns(src, first) for _, _, first in firsts]
    loads[1].wait()
    totals = [None] * len(firsts)
    for i in range(2):
        loads[2 + i].wait()
        at = slice(i * half, (i + 1) * half)
        for n, col in enumerate(cols):
            part = picked(col, (source.at[at, :],), (i * half,))
            totals[n] = part if totals[n] is None else totals[n] + part
    stores = []
    for (which, k, first), total in zip(firsts, totals):
        made[which][k * edges : (k + 1) * edges, :] = scaled(total, weight, first)
        if (k + 1) * edges == made[which].shape[0]:
            stores.append(pltpu.make_async_copy(made[which], outs[which], sems.at[4 + which]))
            stores[-1].start()
    for store in stores:
        store.wait()


def locals_(start, src_ref, weight_ref, sources, bases, out_ref, before_ref, keep_ref, kept_ref):
    edges = STEP * TILE
    count = out_ref.shape[0] // edges
    pair = max(n for n in range(1, 7) if count % n == 0)

    def step(k, carry):
        for i in range(pair):
            n = k * pair + i
            at = pl.ds(pl.multiple_of(n * edges, edges), edges)
            first = start + n * STEP
            cols = columns(src_ref, first) if kept_ref is None else kept_ref[at, :]
            if keep_ref is not None:
                keep_ref[at, :] = cols
            rows = picked(cols, sources, bases)
            if before_ref is not None:
                rows = rows + before_ref[at, :].astype(F32)
            out_ref[at, :] = rows.astype(BF) if weight_ref is None else scaled(rows, weight_ref, first)
        return carry

    lax.fori_loop(0, count // pair, step, 0)


def gather_body(start, src_ref, weight_ref, source_ref, out_ref):
    locals_(start, src_ref, weight_ref, (source_ref,), (0,), out_ref, None, None, None)


def lands(rows_ref, tiles, base, target_rows, there=None):
    spot = lax.broadcasted_iota(jnp.int32, (target_rows, TILE), 0).astype(jnp.int16)
    out = []
    for tile in tiles:
        row = rows_ref[pl.ds(tile, 1), :] - base
        row = row if there is None else jnp.where(there, row, -1)
        row = jnp.broadcast_to(row, (target_rows, TILE)).astype(jnp.int16)
        out.append(jnp.where(row == spot, jnp.ones_like(spot, BF), jnp.zeros_like(spot, BF)))
    return jnp.concatenate(out, axis=1)


def landed(side, dst_ref, first_ref, second_ref, base, target_rows):
    hits, got = [], []
    for which, got_ref in enumerate((first_ref, second_ref)):
        first = outward(which, side)
        tiles = [first + i for i in range(side)]
        hits.append(lands(dst_ref, tiles, base, target_rows, has_partner(which)))
        got.append(got_ref[...])
    return jnp.dot(
        jnp.concatenate(hits, axis=1), jnp.concatenate(got, axis=0), preferred_element_type=F32
    )


def spread_body(side, dst_ref, local_ref, out_ref):
    block = 512

    def step(k, carry):
        for i in range(2):
            at = pl.multiple_of((2 * k + i) * block, block)
            tiles = [2 * side + t for t in range(local_ref.shape[0] // TILE)]
            out_ref[pl.ds(at, block), :] = jnp.dot(
                lands(dst_ref, tiles, at, block), local_ref[...], preferred_element_type=F32
            )
        return carry

    lax.fori_loop(0, out_ref.shape[0] // (2 * block), step, 0)


def start_of(c, b, count):
    return block_of(c, count) * WIN + spot(c, b)


def spread_last_body(side, count, dst_ref, local_ref, *refs):
    hiddens, (out_ref, hidden_ref, sems) = refs[:count], refs[count:]
    copies = []
    for c, chunk_ref in enumerate(hiddens):
        at = pl.ds(pl.multiple_of(block_of(c, count) * WIN, WIN), WIN)
        copies.append(pltpu.make_async_copy(chunk_ref, hidden_ref.at[at, :], sems.at[c]))
        copies[-1].start()
    spread_body(side, dst_ref, local_ref, out_ref)
    for copy in copies:
        copy.wait()


def latent_body(side, c, b, count, dst_ref, first_ref, second_ref, total_ref, embed_ref, out_ref):
    at = pl.multiple_of(start_of(c, b, count), BLOCK)
    got = landed(side, dst_ref, first_ref, second_ref, at, BLOCK)
    got = got + total_ref[pl.ds(at, BLOCK), :]
    out_ref[...] = (embed_ref[pl.ds(at, BLOCK), :].astype(F32) + got).astype(BF)


def grid_body(side, count_ref, dst_ref, first_ref, second_ref, total_ref, grid_ref, out_ref):
    rows = out_ref.shape[0]
    step = pl.program_id(0)
    at = pl.multiple_of(step * rows, rows)
    here = pl.ds(at, rows)
    got = landed(side, dst_ref, first_ref, second_ref, at, rows) + total_ref[here, :]
    row = at + lax.broadcasted_iota(jnp.int32, got.shape, 0)
    value = grid_ref[here, :].astype(F32) + got
    out_ref[...] = jnp.where(row < count_ref[:1, :1], value, 0.0).astype(BF)


def swapped(first, second):
    one, two = partners(lax.axis_size("seq"), lax.axis_size("ens"))
    axes = ("ens", "seq")
    return lax.ppermute(first, axes, one), lax.ppermute(second, axes, two)


def gathered(edge_src, edge_weight, source, side):
    edges = edge_src.shape[0] * TILE - 2 * side * TILE
    (local,) = call(
        functools.partial(gather_body, 2 * side),
        (jax.ShapeDtypeStruct((edges, source.shape[1]), BF),),
        (edge_src, edge_weight, source),
        2 * edges * source.size,
    )
    return local


def spread(edge_dst, local, target_rows, side):
    (total,) = call(
        functools.partial(spread_body, side),
        (jax.ShapeDtypeStruct((target_rows, local.shape[1]), F32),),
        (edge_dst, local),
        2 * local.size * target_rows,
    )
    return total


def settled(side, grid_count, edge_dst, first, second, total, grid_latent):
    rows, features = grid_latent.shape
    block = 512
    args = (grid_count, edge_dst, first, second, total, grid_latent)
    return pl.pallas_call(
        functools.partial(grid_body, side),
        grid=(rows // block,),
        out_shape=jax.ShapeDtypeStruct((rows, features), BF),
        in_specs=[pl.BlockSpec(memory_space=pltpu.VMEM)] * len(args),
        out_specs=pl.BlockSpec((block, features), lambda i: (i, 0)),
        cost_estimate=pl.CostEstimate(
            flops=4 * side * TILE * grid_latent.size,
            bytes_accessed=8 * grid_latent.size,
            transcendentals=0,
        ),
        compiler_params=pltpu.CompilerParams(vmem_limit_bytes=16 * 1024 * 1024),
        name="grid",
    )(*args)


def power(exponent):
    return jnp.where(exponent > 0, 2.0, jnp.where(exponent < 0, 0.5, 1.0)).astype(F32)


def place(step, parts):
    if parts == 1:
        return 0
    mp = lax.axis_index("mp")
    sub = lax.axis_index("sub")
    mp = mp if step < 2 else 1 - mp
    sub = sub if step % 2 == 0 else 1 - sub
    return 2 * mp + sub


def qkv_body(parts, *refs):
    pieces, (gain_ref, w_ref, *refs) = refs[:parts], refs[parts:]
    normed_ref, q_ref, kv_ref = refs
    rows, width = pieces[0].shape
    total = width * parts
    block = min(256, rows)
    lane = lax.broadcasted_iota(jnp.int32, (block, TILE), 1)

    def step(k, carry):
        at = pl.ds(pl.multiple_of(k * block, block), block)
        values = [p[at, :].astype(F32) for p in pieces]
        mean = jnp.sum(sum(values[1:], values[0]), axis=1, keepdims=True) / total
        values = [v - mean for v in values]
        squares = [v * v for v in values]
        var = jnp.sum(sum(squares[1:], squares[0]), axis=1, keepdims=True) / total
        scale = lax.rsqrt(var + 1e-05)
        for i, v in enumerate(values):
            cols = pl.ds(pl.multiple_of(place(i, parts) * width, width), width)
            normed_ref[at, cols] = (v * scale * gain_ref[:, cols]).astype(BF)
        out = jnp.dot(normed_ref[at, :], w_ref[...], preferred_element_type=F32)
        for pair in range(q_ref.shape[1] // TILE):
            a, b, c = [out[:, (3 * pair + i) * TILE : (3 * pair + i + 1) * TILE] for i in range(3)]
            q = pltpu.roll(jnp.where(lane < HD, a, b), HD, 1) * (HD**-0.5 * LOG2E)
            q_ref[at, pair * TILE : (pair + 1) * TILE] = q.astype(BF)
            kv_ref[at, 2 * pair * TILE : (2 * pair + 1) * TILE] = jnp.where(lane < HD, b, a).astype(BF)
            kv_ref[at, (2 * pair + 1) * TILE : (2 * pair + 2) * TILE] = c.astype(BF)
        return carry

    lax.fori_loop(0, rows // block, step, 0)


def up_body(normed_ref, w_ref, exp_ref, out_ref):
    rows = normed_ref.shape[0]
    block = min(256, rows)
    cols = min(512, w_ref.shape[1])

    def step(k, carry):
        at = pl.ds(pl.multiple_of(k * block, block), block)
        for c in range(w_ref.shape[1] // cols):
            sl = slice(c * cols, (c + 1) * cols)
            up = jnp.dot(normed_ref[at, :], w_ref[:, sl], preferred_element_type=F32)
            up = up * power(exp_ref[:, sl])
            out_ref[at, sl] = (0.5 * up * (1.0 + lax.erf(up * 0.7071067811865476))).astype(BF)
        return carry

    lax.fori_loop(0, rows // block, step, 0)


def spot(which, b):
    n = WIN // BLOCK
    return jnp.where(parity() == which, b, n - 1 - b) * BLOCK


def slanted(which):
    i = lax.broadcasted_iota(jnp.int32, (BLOCK, BLOCK), 0)
    j = lax.broadcasted_iota(jnp.int32, (BLOCK, BLOCK), 1)
    return jnp.where(parity() == which, i - j, j - i)


def lane_ids():
    return lax.broadcasted_iota(jnp.int32, (BLOCK, TILE), 1)


def query_of(q_ref, pair, half):
    q = q_ref[:, pair * TILE : (pair + 1) * TILE]
    keep = (lane_ids() >= HD) if half == 0 else (lane_ids() < HD)
    return jnp.where(keep, q, jnp.zeros_like(q))


def scored(q, key):
    return lax.dot_general(q, key, (((1,), (1,)), ((), ())), preferred_element_type=F32)


def peak_of(scores):
    peak = scores[0]
    for s in scores[1:]:
        peak = jnp.maximum(peak, s)
    return jnp.max(peak, axis=1, keepdims=True)


def attend_body(which, b, q_ref, *refs):
    *refs, out_ref = refs
    bias = jnp.where(has_partner(which), 0.0, NEG).astype(F32)
    ahead = slanted(which)
    inner_mask = jnp.where(ahead <= 0, 0.0, NEG).astype(F32)
    outer_mask = jnp.where(ahead >= 0, bias, NEG).astype(F32)
    left = lane_ids() < HD
    jobs = [(pair, half) for pair in range(q_ref.shape[1] // TILE) for half in range(2)]

    def scores_of(pair, half):
        cols = slice((2 * pair + half) * TILE, (2 * pair + half + 1) * TILE)
        q = query_of(q_ref, pair, half)
        keys = [ref[:, cols] for ref in refs]
        scores = [scored(q, key) for key in keys]
        scores[0] = scores[0] + inner_mask
        scores[4] = scores[4] + outer_mask
        if b == 1:
            scores[3] = scores[3] + bias
        return keys, scores

    outs = []
    ready = scores_of(*jobs[0])
    for n, (pair, half) in enumerate(jobs):
        keys, scores = ready
        if n + 1 < len(jobs):
            ready = scores_of(*jobs[n + 1])
        peak = peak_of(scores)
        probs = jnp.concatenate([jnp.exp2(s - peak).astype(BF) for s in scores], axis=1)
        keep = left if half == 0 else jnp.logical_not(left)
        values = [jnp.where(keep, key, jnp.ones_like(key)) for key in keys]
        outs.append(jnp.dot(probs, jnp.concatenate(values, axis=0), preferred_element_type=F32))
        if half:
            sums = pltpu.roll(jnp.where(left, outs[1], outs[0]), HD, 1)
            mixed = jnp.where(left, outs[0], outs[1])
            out_ref[:, pair * TILE : (pair + 1) * TILE] = (mixed / sums).astype(BF)
            outs = []


def down_body(parts, n, *refs):
    atts, acts, (w_out_ref, w_down_ref, exp_ref), outs = (
        refs[:n],
        refs[n : 2 * n],
        refs[2 * n : 2 * n + 3],
        refs[2 * n + 3 :],
    )
    width = w_out_ref.shape[1] // parts
    for k in range(n):
        at = slice(k * BLOCK, (k + 1) * BLOCK)
        for i in range(parts):
            cols = pl.ds(pl.multiple_of(place(i, parts) * width, width), width)
            mlp = jnp.dot(acts[k][...], w_down_ref[:, cols], preferred_element_type=F32)
            att = jnp.dot(atts[k][...], w_out_ref[:, cols], preferred_element_type=F32)
            outs[i][at, :] = (att + mlp * power(exp_ref[:, cols])).astype(BF)


SWAP = [(0, 1), (1, 0)]
PIECES = ((0, 1), (0, 0), (1, 1), (1, 0))
UNITS = ((1, 0), (3,), (2,))


def gather(rows, split):
    if not split:
        return [lax.all_gather(rows, ("mp", "sub"), axis=1, tiled=True)]
    far = lax.ppermute(rows, "mp", SWAP)
    near = lax.ppermute(rows, "sub", SWAP)
    both = lax.ppermute(far, "sub", SWAP)
    return [rows, near, far, both]


def reduce_parts(parts, split):
    if not split:
        return [lax.psum_scatter(parts[0], ("mp", "sub"), scatter_dimension=1, tiled=True)]
    own, near, far, both = parts
    far_got = lax.ppermute(both, "sub", SWAP)
    near_got = lax.ppermute(near, "sub", SWAP)
    far_sum = (far.astype(F32) + far_got.astype(F32)).astype(BF)
    return [own, near_got, lax.ppermute(far_sum, "mp", SWAP)]


def settle_body(unit, *refs):
    n = len(unit)
    latents, (*adds, out) = refs[:n], refs[n:]
    if out.shape[0] > n * BLOCK:
        earlier_ref, *adds = adds
        other = spot(PIECES[unit[0]][0], 1 - PIECES[unit[0]][1])
        out[pl.ds(pl.multiple_of(other, BLOCK), BLOCK), :] = earlier_ref[...]
    for k, g in enumerate(unit):
        at = slice(k * BLOCK, (k + 1) * BLOCK)
        total = adds[0][at, :].astype(F32)
        for term in adds[1:]:
            total = total + term[at, :].astype(F32)
        start = 0 if out.shape[0] == BLOCK else spot(*PIECES[g])
        spots = pl.ds(pl.multiple_of(start, BLOCK), BLOCK) if out.shape[0] > BLOCK else slice(None)
        out[spots, :] = (latents[k][...].astype(F32) + total).astype(BF)


def leave_body(side, c, count, src_ref, *refs):
    last = c == count - 1
    weight_ref, refs = (refs[0], refs[1:]) if last else (None, refs)
    hidden_ref, before, outs = refs[:1], refs[1:-2], refs[-2:]
    sides(side, src_ref, weight_ref, hidden_ref, (block_of(c, count) * WIN,), outs, before or None)


def stay_body(side, c, count, src_ref, *refs):
    base = (block_of(c, count) * WIN,)
    if c == count - 1:
        weight_ref, hidden_ref, before_ref, kept_ref, out_ref = refs
        locals_(
            2 * side, src_ref, weight_ref, (hidden_ref,), base, out_ref, before_ref, None, kept_ref
        )
    else:
        hidden_ref, out_ref, keep_ref = refs
        locals_(2 * side, src_ref, None, (hidden_ref,), base, out_ref, None, keep_ref, None)


def leaving(side, c, count, args, hidden, before):
    out = jax.ShapeDtypeStruct((side * TILE, hidden.shape[1]), BF)
    return call(
        functools.partial(leave_body, side, c, count),
        (out, out),
        (*args, hidden, *before),
        4 * side * TILE * hidden.size,
    )


def staying(side, c, count, args, hidden, before):
    edges = (args[0].shape[0] - 2 * side) * TILE
    outs = [jax.ShapeDtypeStruct((edges, hidden.shape[1]), BF)]
    if not before:
        outs.append(jax.ShapeDtypeStruct((edges, TILE), jnp.int16))
    return call(
        functools.partial(stay_body, side, c, count),
        outs,
        (*args, hidden, *before),
        2 * edges * hidden.size,
    )


def shards(
    grid_latent,
    grid_count,
    hidden_embed,
    enc_src_rows,
    enc_dst_rows,
    enc_weight,
    dec_src_rows,
    dec_dst_rows,
    dec_weight,
    norm_gain,
    w_qkv,
    w_out,
    w_up,
    up_exp,
    w_down,
    down_exp,
):
    split = lax.axis_size("mp") == 2 and lax.axis_size("sub") == 2
    parts = 4 if split else 1
    hid_rows, features = hidden_embed.shape
    full = w_qkv.shape[0]
    heads = w_qkv.shape[1] // (3 * HD)
    units = w_up.shape[1]
    rows = WIN
    count = hid_rows // rows
    assert count == 2
    src, dst, wts = enc_src_rows[0], enc_dst_rows[0], enc_weight[0]
    out = jax.ShapeDtypeStruct((ESIDE * TILE, features), BF)
    args = (src, wts, grid_latent)
    out = call(
        functools.partial(fetch_side_body, ESIDE),
        (out, out),
        args,
        4 * ESIDE * TILE * grid_latent.size,
        scratch=[
            *(pltpu.VMEM(a.shape, a.dtype) for a in (*args, out, out)),
            pltpu.SemaphoreType.DMA((6,)),
        ],
        space=pltpu.HBM,
        out_space=pltpu.HBM,
        limit=60 * 1024 * 1024,
    )
    arrived = swapped(*out)
    moved = gathered(src, wts, grid_latent, ESIDE)
    total = spread(dst, moved, hid_rows, ESIDE)
    latents, gathers = [], []
    for c, b in PIECES:
        (latent,) = call(
            functools.partial(latent_body, ESIDE, c, b, count),
            (jax.ShapeDtypeStruct((BLOCK, features), BF),),
            (dst, *arrived, total, hidden_embed),
            4 * ESIDE * TILE * BLOCK * features,
        )
        latents.append(latent)
        gathers.append(gather(latent, split))
    links = partners(lax.axis_size("seq"), lax.axis_size("ens"))
    queries, kvs, outer, activated = [], [], [], []
    for g, (c, b) in enumerate(PIECES):
        normed, q, part = call(
            functools.partial(qkv_body, parts),
            (
                jax.ShapeDtypeStruct((BLOCK, full), BF),
                jax.ShapeDtypeStruct((BLOCK, heads * HD), BF),
                jax.ShapeDtypeStruct((BLOCK, 2 * heads * HD), BF),
            ),
            (*gathers[g], norm_gain[None, :], w_qkv),
            2 * BLOCK * w_qkv.size,
        )
        queries.append(q)
        kvs.append(part)
        outer.append(lax.ppermute(part, ("ens", "seq"), links[c]))
        (act,) = call(
            up_body,
            (jax.ShapeDtypeStruct((BLOCK, units), BF),),
            (normed, w_up, up_exp[None, :]),
            2 * BLOCK * w_up.size,
        )
        activated.append(act)
    attended = []
    for g, (c, b) in enumerate(PIECES):
        o, h = 2 * (1 - c), 2 * c
        keys = (kvs[o], kvs[o + 1], kvs[h + 1], kvs[h], outer[h], outer[h + 1])[b : b + 5]
        (att,) = call(
            functools.partial(attend_body, c, b),
            (jax.ShapeDtypeStruct((BLOCK, heads * HD), BF),),
            (queries[g], *keys),
            4 * BLOCK * 5 * BLOCK * heads * HD,
            spare=12,
        )
        attended.append(att)
    src, dst, wts = dec_src_rows[0], dec_dst_rows[0], dec_weight[0]
    hiddens = []
    for u, unit in enumerate(UNITS):
        size = len(unit) * BLOCK
        outs = call(
            functools.partial(down_body, parts, len(unit)),
            [jax.ShapeDtypeStruct((size, full // parts), BF)] * parts,
            (
                *(attended[g] for g in unit),
                *(activated[g] for g in unit),
                w_out,
                w_down,
                down_exp[None, :],
            ),
            2 * size * (w_out.size + w_down.size),
        )
        sums = reduce_parts(outs, split)
        earlier = hiddens[-1:] if u == len(UNITS) - 1 else []
        (hidden,) = call(
            functools.partial(settle_body, unit),
            (jax.ShapeDtypeStruct((size + len(earlier) * BLOCK, features), BF),),
            (*(latents[g] for g in unit), *earlier, *sums),
            4 * size * features,
        )
        hiddens.append(hidden)
    hiddens = [hiddens[0], hiddens[-1]]
    before = leaving(DSIDE, 0, count, (src,), hiddens[0], ())
    kept = staying(DSIDE, 0, count, (src,), hiddens[0], ())
    args = (src, wts)
    arrived = swapped(*leaving(DSIDE, 1, count, args, hiddens[1], before))
    (moved,) = staying(DSIDE, 1, count, args, hiddens[1], kept)
    total, hidden_out = call(
        functools.partial(spread_last_body, DSIDE, count),
        (
            jax.ShapeDtypeStruct(grid_latent.shape, F32),
            jax.ShapeDtypeStruct(hidden_embed.shape, BF),
        ),
        (dst, moved, *hiddens),
        2 * moved.size * grid_latent.shape[0],
        scratch=[pltpu.SemaphoreType.DMA((count,))],
        last_space=pltpu.HBM,
    )
    live = jnp.broadcast_to(grid_count[None, :], (8, TILE))
    return hidden_out, settled(DSIDE, live, dst, *arrived, total, grid_latent)


def solution(mesh):
    placed = (
        P(("ens", "seq"), ("mp", "sub")),
        P(("ens", "seq")),
        P(("ens", "seq"), ("mp", "sub")),
        P(("ens", "seq"), None, None),
        P(("ens", "seq"), None, None),
        P(("ens", "seq"), None, None),
        P(("ens", "seq"), None, None),
        P(("ens", "seq"), None, None),
        P(("ens", "seq"), None, None),
        P(),
        P(None, ("mp", "sub")),
        P(("mp", "sub"), None),
        P(None, ("mp", "sub")),
        P(("mp", "sub")),
        P(("mp", "sub"), None),
        P(),
    )
    return jax.shard_map(
        shards,
        mesh=mesh,
        in_specs=placed,
        out_specs=(P(("ens", "seq"), ("mp", "sub")), P(("ens", "seq"), ("mp", "sub"))),
        check_vma=False,
    )
```
